32 devices in a mesh: seq: 8 (over z, y), fsdp: 4 (over x, core).
Axes of the slice: x: 2, y: 2, z: 4, core: 2. Of those that a mesh axis runs over, the one named last changes fastest.
Arguments:
- block_in: bfloat16 [8192, 768], P(('seq', 'fsdp')), may hold values from -6 to 6
- seq_ids: int32 [8192], P(('seq', 'fsdp')), may hold values from 0 to 2, as said below
- positions: int32 [8192], P(('seq', 'fsdp')), may hold values from 0 to 8191, as said below
- attn_gain: bfloat16 [768], P('fsdp'), may hold values from 0.5 to 1.5
- qkv_weight: bfloat16 [768, 2304], P('fsdp'), may hold values from -0.21875 to 0.21875
- attn_out_weight: bfloat16 [768, 768], P('fsdp'), may hold values from -2.5 to 2.5
- mlp_gain: bfloat16 [768], P('fsdp'), may hold values from 0.5 to 1.5
- mlp_in_weight: bfloat16 [768, 2304], P('fsdp'), may hold values from -0.21875 to 0.21875
- mlp_out_weight: bfloat16 [1152, 768], P('fsdp'), may hold values from -0.1875 to 0.1875
- cotangent: bfloat16 [8192, 768], P(('seq', 'fsdp')), may hold values from -6 to 6
Outputs:
- block_out: bfloat16 [8192, 768], P(('seq', 'fsdp'))
- input_grad: float32 [8192, 768], P(('seq', 'fsdp'))
- attn_gain_grad: float32 [768], P('fsdp')
- qkv_weight_grad: float32 [768, 2304], P('fsdp')
- attn_out_weight_grad: float32 [768, 768], P('fsdp')
- mlp_gain_grad: float32 [768], P('fsdp')
- mlp_in_weight_grad: float32 [768, 2304], P('fsdp')
- mlp_out_weight_grad: float32 [1152, 768], P('fsdp')
The draws below stay inside these ranges and needn't reach their ends.
Inputs may be any that keep to these rules, and one draw needn't show every extreme that they name: seq_ids never fall from token to token and take every value of 0 to 2; each sequence holds 1024 tokens or more. Within a sequence positions rise by one from token to token; the first token of all has position 0 and the last token of all has position 8191.
All inputs are finite; a program needn't handle non-finite values.
Results may differ from the reference program's by a relative error of at most 0.018.
Values may be sent and summed in bfloat16 or wider, within the bound.
A program may use at most 192 MiB of HBM per device.

```python
import jax
import jax.numpy as jnp
from jax import lax

D = 768
H = 12
HD = 64
FF = 1152
W = 64
TOK_DEV = 256
TOKENS = 8192


def sequence_layout(base_key):
    first_key = jax.random.fold_in(base_key, 101)
    second_key = jax.random.fold_in(base_key, 202)
    shift_key = jax.random.fold_in(base_key, 303)
    cut_one = jax.random.randint(first_key, (), TOKENS // 4, TOKENS // 2)
    cut_two = jax.random.randint(second_key, (), TOKENS // 2 + TOKENS // 8, TOKENS - TOKENS // 8 + 1)
    index_rows = jnp.arange(TOKENS, dtype=jnp.int32)
    ids_rows = (index_rows >= cut_one).astype(jnp.int32) + (index_rows >= cut_two).astype(jnp.int32)
    starts = jnp.stack([jnp.zeros((), jnp.int32), cut_one.astype(jnp.int32), cut_two.astype(jnp.int32)])
    middle_shift = jax.random.randint(shift_key, (1,), 0, TOKENS // 8).astype(jnp.int32)
    shifts = jnp.concatenate([jnp.zeros((1,), jnp.int32), middle_shift, cut_two.astype(jnp.int32)[None]])
    pos_rows = shifts[ids_rows] + index_rows - starts[ids_rows]
    return (ids_rows, pos_rows)


def draw_seq_ids(key, part):
    return sequence_layout(key)[0]


def draw_positions(key, part):
    return sequence_layout(key)[1]


def block_levels(rng, shape, split, least, top_value):
    loudness, own = 1.0, jax.random.fold_in(rng, 6)
    for axis_at, blocks in split:
        draws = jnp.exp(jax.random.uniform(jax.random.fold_in(own, axis_at), (blocks,), jnp.float32, least / len(split), top_value / len(split)))
        loudness = loudness * jnp.repeat(draws, shape[axis_at] // blocks).reshape([-1 if axis == axis_at else 1 for axis in range(len(shape))])
    return loudness


def noise(rng, shape, spread, reach, pieces=(), held_as=jnp.bfloat16):
    loudness = block_levels(rng, shape, pieces, -0.22, 0.18) if pieces else 1.0
    values = jax.random.normal(rng, shape, jnp.float32) * spread * loudness
    return jnp.minimum(jnp.maximum(values, -reach), reach).astype(held_as)


def setup_inputs(seed: int = 0) -> dict:
    key_list = jax.random.split(jax.random.key(seed), 11)
    block_in = noise(key_list[0], (TOKENS, D), 1.0, 6.0, ((0, 32),))
    seq_ids = draw_seq_ids(jax.random.fold_in(key_list[10], 71), 0)
    positions = draw_positions(jax.random.fold_in(key_list[10], 71), 0)
    attn_gain = jnp.clip(1.0 + 0.1 * jax.random.normal(key_list[3], (D,), jnp.float32), 0.5, 1.5).astype(jnp.bfloat16)
    qkv_weight = noise(key_list[4], (D, 3 * D), D ** -0.5, 0.21875, ((0, 4),))
    attn_out_weight = noise(key_list[5], (D, D), (D // (2 * W)) ** -0.5, 2.5, ((0, 4),))
    mlp_gain = jnp.clip(1.0 + 0.1 * jax.random.normal(key_list[6], (D,), jnp.float32), 0.5, 1.5).astype(jnp.bfloat16)
    mlp_in_weight = noise(key_list[7], (D, 2 * FF), D ** -0.5, 0.21875, ((0, 4),))
    mlp_out_weight = noise(key_list[8], (FF, D), FF ** -0.5, 0.1875, ((0, 4),))
    cotangent = noise(key_list[9], (TOKENS, D), 1.0, 6.0, ((0, 32),))
    return dict(block_in=block_in, seq_ids=seq_ids, positions=positions, attn_gain=attn_gain, qkv_weight=qkv_weight, attn_out_weight=attn_out_weight, mlp_gain=mlp_gain, mlp_in_weight=mlp_in_weight, mlp_out_weight=mlp_out_weight, cotangent=cotangent)


epsilon = 1e-05
rope_base = 10000.0

def norm_forward(inputs):
    center = inputs - lax.optimization_barrier(jnp.mean(inputs, axis=-1, keepdims=True))
    inverse = lax.rsqrt(lax.optimization_barrier(jnp.mean(center * center, axis=-1, keepdims=True)) + epsilon)
    return (center * inverse, inverse)

def norm_backward(grad_hat, normed, inverse):
    mean_grad = lax.optimization_barrier(jnp.mean(grad_hat, axis=-1, keepdims=True))
    mean_cross = lax.optimization_barrier(jnp.mean(grad_hat * normed, axis=-1, keepdims=True))
    return inverse * (grad_hat - mean_grad - normed * mean_cross)

def rotation(token_pos, head_dim):
    half_dim = head_dim // 2
    frequency = rope_base ** (-(jnp.arange(half_dim, dtype=jnp.float32) * 2.0 / head_dim))
    angles = token_pos.astype(jnp.float32)[:, None] * frequency[None, :]
    return (jnp.cos(angles)[:, None, :], jnp.sin(angles)[:, None, :])

def rotate(inputs, cosine_part, sine_part):
    half_dim = inputs.shape[-1] // 2
    upper = inputs[..., :half_dim]
    lower = inputs[..., half_dim:]
    return jnp.concatenate([upper * cosine_part - lower * sine_part, lower * cosine_part + upper * sine_part], axis=-1)

def unrotate(grads, cosine_part, sine_part):
    half_dim = grads.shape[-1] // 2
    upper = grads[..., :half_dim]
    lower = grads[..., half_dim:]
    return jnp.concatenate([upper * cosine_part + lower * sine_part, lower * cosine_part - upper * sine_part], axis=-1)

def gelu_parts(pre_act):
    normal_cdf = 0.5 * (1.0 + lax.erf(pre_act * 0.7071067811865476))
    normal_pdf = jnp.exp(-0.5 * pre_act * pre_act) * 0.3989422804014327
    return (pre_act * normal_cdf, normal_cdf + pre_act * normal_pdf)

def band_mask(query_ids, key_ids):
    query_count = query_ids.shape[0]
    key_count = key_ids.shape[0]
    window_reach = (key_count - query_count) // 2
    offsets = jnp.arange(query_count)[:, None] + window_reach - jnp.arange(key_count)[None, :]
    return (jnp.abs(offsets) <= window_reach) & (query_ids[:, None] == key_ids[None, :])

def mix(form, left, right):
    return jnp.einsum(form, left.astype(jnp.float32), right.astype(jnp.float32))

def attend_ref(queries, key_rows, value_rows, allowed):
    score_scale = HD ** (-0.5)
    scores = mix('qhd,khd->hqk', queries, key_rows) * score_scale
    scores = jnp.where(allowed[None], scores, -1e+30)
    log_total = jnp.log(lax.optimization_barrier(jnp.sum(jnp.exp(scores), axis=-1)))
    attn_probs = jnp.exp(scores - log_total[..., None]).astype(jnp.bfloat16)
    return (mix('hqk,khd->qhd', attn_probs, value_rows), log_total)

def attend_back_ref(queries, key_rows, value_rows, allowed, log_total, grad_out):
    score_scale = HD ** (-0.5)
    scores = mix('qhd,khd->hqk', queries, key_rows) * score_scale
    probs_full = jnp.where(allowed[None], jnp.exp(scores - log_total[..., None]), 0.0)
    grad_probs = mix('qhd,khd->hqk', grad_out, value_rows)
    row_delta = lax.optimization_barrier(jnp.sum(probs_full * grad_probs, axis=-1, keepdims=True))
    grad_scores = (probs_full * (grad_probs - row_delta) * score_scale).astype(jnp.bfloat16)
    grad_query = mix('hqk,khd->qhd', grad_scores, key_rows)
    grad_keys = mix('hqk,qhd->khd', grad_scores, queries)
    grad_values = mix('hqk,qhd->khd', probs_full.astype(jnp.bfloat16), grad_out)
    return (grad_query, grad_keys, grad_values)

def reference(block_in, seq_ids, positions, attn_gain, qkv_weight, attn_out_weight, mlp_gain, mlp_in_weight, mlp_out_weight, cotangent):
    block_rows = TOK_DEV * 4
    blocks = TOKENS // block_rows
    ext_rows = block_rows + 2 * W
    gain_one = attn_gain.astype(jnp.float32)
    gain_two = mlp_gain.astype(jnp.float32)
    indices = jnp.arange(blocks, dtype=jnp.int32)

    def first_norm(index):
        begin_at = (index * block_rows).astype(jnp.int32)
        inputs = lax.dynamic_slice_in_dim(block_in, begin_at, block_rows, 0).astype(jnp.float32)
        token_pos = lax.dynamic_slice_in_dim(positions, begin_at, block_rows, 0)
        normed, inverse = norm_forward(inputs)
        cosine_part, sine_part = rotation(token_pos, HD)
        return (inputs, normed, inverse, cosine_part, sine_part)

    def project(index):
        inputs, normed, inverse, cosine_part, sine_part = first_norm(index)
        normed_in = (normed * gain_one).astype(jnp.bfloat16)
        packed_qkv = jnp.dot(normed_in, qkv_weight, preferred_element_type=jnp.float32)
        queries = rotate(packed_qkv[:, :D].reshape(block_rows, H, HD), cosine_part, sine_part).astype(jnp.bfloat16)
        key_rows = rotate(packed_qkv[:, D:2 * D].reshape(block_rows, H, HD), cosine_part, sine_part).astype(jnp.bfloat16)
        value_rows = packed_qkv[:, 2 * D:].astype(jnp.bfloat16)
        return (queries.reshape(block_rows, D), key_rows.reshape(block_rows, D), value_rows)
    queries_all, keys_all, values_all = lax.map(project, indices)
    queries_all = queries_all.reshape(TOKENS, D)
    keys_pad = jnp.pad(keys_all.reshape(TOKENS, D), ((W, W), (0, 0)))
    values_pad = jnp.pad(values_all.reshape(TOKENS, D), ((W, W), (0, 0)))
    ids_pad = jnp.pad(seq_ids + 1, (W, W))

    def forward_back(carry, index):
        sum_gain_two, sum_in, sum_out, sum_attn_out = carry
        begin_at = (index * block_rows).astype(jnp.int32)
        inputs = lax.dynamic_slice_in_dim(block_in, begin_at, block_rows, 0).astype(jnp.float32)
        grad_in = lax.dynamic_slice_in_dim(cotangent, begin_at, block_rows, 0)
        queries = lax.dynamic_slice_in_dim(queries_all, begin_at, block_rows, 0).reshape(block_rows, H, HD)
        key_rows = lax.dynamic_slice_in_dim(keys_pad, begin_at, ext_rows, 0).reshape(ext_rows, H, HD)
        value_rows = lax.dynamic_slice_in_dim(values_pad, begin_at, ext_rows, 0).reshape(ext_rows, H, HD)
        key_ids = lax.dynamic_slice_in_dim(ids_pad, begin_at, ext_rows, 0)
        query_ids = lax.dynamic_slice_in_dim(seq_ids, begin_at, block_rows, 0) + 1
        allowed = band_mask(query_ids, key_ids)
        attn_out, log_total = attend_ref(queries, key_rows, value_rows, allowed)
        attn_flat = attn_out.reshape(block_rows, D).astype(jnp.bfloat16)
        hidden_one = inputs + jnp.dot(attn_flat, attn_out_weight, preferred_element_type=jnp.float32)
        normed_two, inverse_two = norm_forward(hidden_one)
        normed_mid = (normed_two * gain_two).astype(jnp.bfloat16)
        up_rows = jnp.dot(normed_mid, mlp_in_weight, preferred_element_type=jnp.float32)
        gelu_value, gelu_slope = gelu_parts(up_rows[:, :FF])
        gate_rows = up_rows[:, FF:]
        mixed = (gelu_value * gate_rows).astype(jnp.bfloat16)
        block_rows_out = (hidden_one + jnp.dot(mixed, mlp_out_weight, preferred_element_type=jnp.float32)).astype(jnp.bfloat16)
        grad_mixed = jnp.dot(grad_in, mlp_out_weight.T, preferred_element_type=jnp.float32)
        grad_up = jnp.concatenate([grad_mixed * gate_rows * gelu_slope, grad_mixed * gelu_value], axis=1).astype(jnp.bfloat16)
        grad_normed_two = jnp.dot(grad_up, mlp_in_weight.T, preferred_element_type=jnp.float32)
        grad_hidden = grad_in.astype(jnp.float32) + norm_backward(grad_normed_two * gain_two, normed_two, inverse_two)
        grad_hidden_b = grad_hidden.astype(jnp.bfloat16)
        grad_attn = jnp.dot(grad_hidden_b, attn_out_weight.T, preferred_element_type=jnp.float32).astype(jnp.bfloat16)
        grad_query, grad_keys, grad_values = attend_back_ref(queries, key_rows, value_rows, allowed, log_total, grad_attn.reshape(block_rows, H, HD))
        sum_gain_two = sum_gain_two + lax.optimization_barrier(jnp.sum(grad_normed_two * normed_two, axis=0))
        sum_in = sum_in + jnp.dot(normed_mid.T, grad_up, preferred_element_type=jnp.float32)
        sum_out = sum_out + jnp.dot(mixed.T, grad_in, preferred_element_type=jnp.float32)
        sum_attn_out = sum_attn_out + jnp.dot(attn_flat.T, grad_hidden_b, preferred_element_type=jnp.float32)
        key_grads = jnp.concatenate([grad_keys.reshape(ext_rows, D), grad_values.reshape(ext_rows, D)], axis=1)
        return ((sum_gain_two, sum_in, sum_out, sum_attn_out), (block_rows_out, grad_hidden, grad_query.reshape(block_rows, D), key_grads))
    start_carry = (jnp.zeros((D,), jnp.float32), jnp.zeros((D, 2 * FF), jnp.float32), jnp.zeros((FF, D), jnp.float32), jnp.zeros((D, D), jnp.float32))
    sums_mid, stacked = lax.scan(forward_back, start_carry, indices)
    mlp_gain_grad, mlp_in_weight_grad, mlp_out_weight_grad, attn_out_weight_grad = sums_mid
    outputs, grads_hidden, grads_query, key_grads = stacked
    inner = key_grads[:, W:W + block_rows]
    before_part = key_grads[:, :W]
    after_part = key_grads[:, W + block_rows:]
    zero_edge = jnp.zeros_like(before_part[:1])
    from_next = jnp.concatenate([before_part[1:], zero_edge], axis=0)
    from_prev = jnp.concatenate([zero_edge, after_part[:-1]], axis=0)
    inner = inner.at[:, block_rows - W:].add(from_next).at[:, :W].add(from_prev)

    def input_side(carry, packed_in):
        sum_gain_one, sum_qkv = carry
        index, grad_hidden, grad_query, key_grad_rows = packed_in
        inputs, normed, inverse, cosine_part, sine_part = first_norm(index)
        normed_in = (normed * gain_one).astype(jnp.bfloat16)
        grad_q = unrotate(grad_query.reshape(block_rows, H, HD), cosine_part, sine_part).reshape(block_rows, D)
        grad_k = unrotate(key_grad_rows[:, :D].reshape(block_rows, H, HD), cosine_part, sine_part).reshape(block_rows, D)
        grad_qkv = jnp.concatenate([grad_q, grad_k, key_grad_rows[:, D:]], axis=1).astype(jnp.bfloat16)
        sum_qkv = sum_qkv + jnp.dot(normed_in.T, grad_qkv, preferred_element_type=jnp.float32)
        grad_normed = jnp.dot(grad_qkv, qkv_weight.T, preferred_element_type=jnp.float32)
        sum_gain_one = sum_gain_one + lax.optimization_barrier(jnp.sum(grad_normed * normed, axis=0))
        grad_input = grad_hidden + norm_backward(grad_normed * gain_one, normed, inverse)
        return ((sum_gain_one, sum_qkv), grad_input)
    sums_low, grads_input = lax.scan(input_side, (jnp.zeros((D,), jnp.float32), jnp.zeros((D, 3 * D), jnp.float32)), (indices, grads_hidden, grads_query, inner))
    attn_gain_grad, qkv_weight_grad = sums_low
    return (outputs.reshape(TOKENS, D), grads_input.reshape(TOKENS, D), attn_gain_grad, qkv_weight_grad, attn_out_weight_grad, mlp_gain_grad, mlp_in_weight_grad, mlp_out_weight_grad)
```

```python
import functools

import jax
import jax.numpy as jnp
from jax import lax
from jax.experimental import pallas as pl
from jax.experimental.pallas import tpu as pltpu
from jax.sharding import PartitionSpec as P

HD = 64
W = 64


epsilon = 1e-05
rope_base = 10000.0


def shifted(array, axis, by):
    size = lax.axis_size(axis)
    pairs = [(i, i + by) for i in range(size) if 0 <= i + by < size]
    return lax.ppermute(array, axis, pairs)


def places():
    fsdp_at = lax.axis_index("fsdp")
    seq_at = lax.axis_index("seq")
    chip_x = fsdp_at // 2
    core = lax.rem(fsdp_at, 2)
    return fsdp_at, seq_at, chip_x, core


def flipped(index, bit):
    flag = lax.rem(index // bit, 2)
    return index + bit - 2 * bit * flag


def greet(partners):
    barrier = pltpu.get_barrier_semaphore()
    for name, at in partners:
        pl.semaphore_signal(
            barrier, inc=1, device_id={name: at}, device_id_type=pl.DeviceIdType.MESH
        )
    pl.semaphore_wait(barrier, len(partners))


def remote(src, dst, send, recv, name, at):
    return pltpu.make_async_remote_copy(
        src_ref=src,
        dst_ref=dst,
        send_sem=send,
        recv_sem=recv,
        device_id={name: at},
        device_id_type=pl.DeviceIdType.MESH,
    )


def gather_kernel(count, *refs):
    shards = refs[:count]
    wholes = refs[count : 2 * count]
    send, recv, local_sem = refs[2 * count :]
    fsdp_at, seq_at, chip_x, core = places()
    side = lax.rem(seq_at, 2)
    beside = flipped(fsdp_at, 1)
    across = flipped(fsdp_at, 2)
    far = flipped(across, 1)
    next_y = flipped(seq_at, 1)
    greet((("fsdp", beside), ("fsdp", across), ("seq", next_y)))

    def rows_of(k, owner, half):
        rows = shards[k].shape[0]
        if half is None:
            return wholes[k].at[pl.ds(pl.multiple_of(owner * rows, 16), rows)]
        begin = owner * rows + half * (rows // 2)
        return wholes[k].at[pl.ds(pl.multiple_of(begin, 16), rows // 2)]

    def mine(k):
        rows = shards[k].shape[0] // 2
        return shards[k].at[pl.ds(pl.multiple_of(side * rows, 16), rows)]

    copies = []
    x_copies = []
    for k in range(count):
        copy = remote(
            mine(k), rows_of(k, fsdp_at, side), send.at[k, 0], recv.at[k, 0], "fsdp", across
        )
        copy.start()
        x_copies.append(copy)
    for k in range(count):
        copy = remote(
            shards[k], rows_of(k, fsdp_at, None), send.at[k, 1], recv.at[k, 1], "fsdp", beside
        )
        copy.start()
        copies.append(copy)
    for k in range(count):
        pltpu.make_async_copy(shards[k], rows_of(k, fsdp_at, None), local_sem.at[k]).start()
    y_copies = []

    def pass_on(k):
        y_copies[k].wait_recv()
        half = rows_of(k, across, 1 - side)
        copy = remote(half, half, send.at[k, 4], recv.at[k, 4], "fsdp", beside)
        copy.start()
        copies.append(copy)

    for k in range(count):
        x_copies[k].wait_recv()
        half = rows_of(k, across, side)
        copy = remote(half, half, send.at[k, 2], recv.at[k, 2], "seq", next_y)
        copy.start()
        y_copies.append(copy)
        copy = remote(half, half, send.at[k, 3], recv.at[k, 3], "fsdp", beside)
        copy.start()
        copies.append(copy)
        if k > 0:
            pass_on(k - 1)
    pass_on(count - 1)
    for k in range(count):
        pltpu.make_async_copy(shards[k], rows_of(k, fsdp_at, None), local_sem.at[k]).wait()
    for copy in copies:
        copy.wait()
    for copy in x_copies + y_copies:
        copy.wait_send()


def gather_all(shards):
    count = len(shards)
    vmem = pl.BlockSpec(memory_space=pltpu.VMEM)
    return pl.pallas_call(
        functools.partial(gather_kernel, count),
        out_shape=[
            jax.ShapeDtypeStruct((4 * shard.shape[0], shard.shape[1]), shard.dtype)
            for shard in shards
        ],
        in_specs=[vmem] * count,
        out_specs=[vmem] * count,
        scratch_shapes=[
            pltpu.SemaphoreType.DMA((count, 5)),
            pltpu.SemaphoreType.DMA((count, 5)),
            pltpu.SemaphoreType.DMA((count,)),
        ],
        compiler_params=pltpu.CompilerParams(
            collective_id=0, has_side_effects=True, vmem_limit_bytes=40 << 20
        ),
        name="gather_all",
    )(*shards)


def add_into(dst, left, right):
    rows = dst.shape[0]
    block = 48 if rows % 48 == 0 else 16

    def step(i, carry):
        at = pl.ds(pl.multiple_of(i * block, 16), block)
        total = left[at].astype(jnp.float32) + right[at].astype(jnp.float32)
        dst[at] = total.astype(dst.dtype)
        return carry

    lax.fori_loop(0, rows // block, step, 0)


def reduce_kernel(chunks, outputs, bits, *refs):
    inputs = max(chunk[0] for chunk in chunks) + 1
    ins = refs[:inputs]
    outs = refs[inputs : inputs + outputs]
    rest = refs[inputs + outputs :]
    n = len(chunks)
    from_core = rest[:n]
    from_x = rest[n : 2 * n]
    from_y = rest[2 * n : 3 * n]
    from_z = rest[3 * n : 4 * n]
    from_far = rest[4 * n : 5 * n]
    final = rest[5 * n : 6 * n]
    send, recv = rest[6 * n :]
    fsdp_at, seq_at, chip_x, core = places()
    y = lax.rem(seq_at, 2)
    z = lax.rem(seq_at // 2, 2)
    beside = flipped(fsdp_at, 1)
    across = flipped(fsdp_at, 2)
    next_y = flipped(seq_at, 1)
    next_z = flipped(seq_at, 2)
    far = [flipped(seq_at, bit) for bit in bits]
    greet(
        [("fsdp", beside), ("fsdp", across), ("seq", next_y), ("seq", next_z)]
        + [("seq", at) for at in far]
    )

    def owner_rows(k, owner):
        source, begin, columns, rows = chunks[k][:4]
        at = pl.ds(pl.multiple_of(owner * rows, 16), rows)
        return ins[source].at[at, pl.ds(begin, columns)]

    def y_half(ref, flag):
        rows = ref.shape[0] // 2
        return ref.at[pl.ds(pl.multiple_of(flag * rows, 16), rows)]

    def z_half(ref, flag):
        rows, columns = ref.shape
        if rows % 32 == 0:
            return ref.at[pl.ds(pl.multiple_of(flag * (rows // 2), 16), rows // 2)]
        return ref.at[:, pl.ds(pl.multiple_of(flag * (columns // 2), 128), columns // 2)]

    started = []
    arriving = {}

    def go(k, slot, src, dst, name, at):
        copy = remote(src, dst, send.at[k, slot], recv.at[k, slot], name, at)
        copy.start()
        started.append(copy)
        arriving[k, slot] = copy

    def core_send(k):
        for far_x in range(2):
            go(
                k, far_x, owner_rows(k, 2 * far_x + 1 - core), from_core[k].at[far_x],
                "fsdp", beside,
            )

    def x_send(k):
        for far_x in range(2):
            arriving[k, far_x].wait_recv()
            spot = from_core[k].at[far_x]
            add_into(spot, spot, owner_rows(k, 2 * far_x + core))
        go(k, 2, from_core[k].at[1 - chip_x], from_x[k], "fsdp", across)

    def y_send(k):
        arriving[k, 2].wait_recv()
        add_into(from_x[k], from_x[k], from_core[k].at[chip_x])
        go(k, 3, y_half(from_x[k], 1 - y), from_y[k], "seq", next_y)

    def z_send(k):
        arriving[k, 3].wait_recv()
        add_into(from_y[k], from_y[k], y_half(from_x[k], y))
        go(k, 4, z_half(from_y[k], 1 - z), from_z[k], "seq", next_z)

    def spot(k):
        return z_half(y_half(final[k], y), z)

    def far_send(level):
        def stage(k):
            if level == 0:
                arriving[k, 4].wait_recv()
                source = from_z[k]
                add_into(source, source, z_half(from_y[k], z))
            else:
                arriving[k, 6 + level].wait_recv()
                source = from_far[k].at[level - 1]
                before = from_z[k] if level == 1 else from_far[k].at[level - 2]
                add_into(source, source, before)
            go(k, 7 + level, source, from_far[k].at[level], "seq", far[level])

        return stage

    def z_back(k):
        if bits:
            level = len(bits) - 1
            arriving[k, 7 + level].wait_recv()
            before = from_z[k] if level == 0 else from_far[k].at[level - 1]
            add_into(spot(k), from_far[k].at[level], before)
        else:
            arriving[k, 4].wait_recv()
            add_into(spot(k), from_z[k], z_half(from_y[k], z))
        go(k, 5, spot(k), spot(k), "seq", next_z)

    def y_back(k):
        arriving[k, 5].wait_recv()
        half = y_half(final[k], y)
        go(k, 6, half, half, "seq", next_y)

    def finish(k):
        arriving[k, 6].wait_recv()
        out, begin, columns = chunks[k][4], chunks[k][5], chunks[k][2]
        rows = outs[out].shape[0]
        block = 48 if rows % 48 == 0 else 16

        def step(i, carry):
            at = pl.ds(pl.multiple_of(i * block, 16), block)
            outs[out][at, pl.ds(begin, columns)] = final[k][at].astype(jnp.float32)
            return carry

        lax.fori_loop(0, rows // block, step, 0)

    stages = [y_send, z_send] + [far_send(i) for i in range(len(bits))] + [z_back, y_back, finish]
    for k in range(n):
        core_send(k)
    for wave in range(n + len(stages) + 1):
        if wave < n:
            x_send(wave)
        for lag in reversed(range(len(stages))):
            k = wave - 2 - lag
            if 0 <= k < n:
                stages[lag](k)
    for copy in started:
        copy.wait_send()


def reduce_all(terms, out_shapes, chunks):
    seq_size = lax.axis_size("seq")
    assert lax.axis_size("fsdp") == 4 and seq_size >= 4 and seq_size & (seq_size - 1) == 0
    bits = []
    while (4 << len(bits)) < seq_size:
        bits.append(4 << len(bits))
    n = len(chunks)
    vmem = pl.BlockSpec(memory_space=pltpu.VMEM)
    halves = []
    quarters = []
    for chunk in chunks:
        columns, rows = chunk[2], chunk[3]
        halves.append((rows // 2, columns))
        quarters.append((rows // 4, columns) if rows % 64 == 0 else (rows // 2, columns // 2))
    scratch = (
        [pltpu.VMEM((2, c[3], c[2]), jnp.bfloat16) for c in chunks]
        + [pltpu.VMEM((c[3], c[2]), jnp.bfloat16) for c in chunks]
        + [pltpu.VMEM(h, jnp.bfloat16) for h in halves]
        + [pltpu.VMEM(q, jnp.bfloat16) for q in quarters]
        + [pltpu.VMEM((max(len(bits), 1),) + q, jnp.bfloat16) for q in quarters]
        + [pltpu.VMEM((c[3], c[2]), jnp.bfloat16) for c in chunks]
        + [pltpu.SemaphoreType.DMA((n, 7 + len(bits)))] * 2
    )
    return pl.pallas_call(
        functools.partial(reduce_kernel, chunks, len(out_shapes), bits),
        out_shape=[jax.ShapeDtypeStruct(shape, jnp.float32) for shape in out_shapes],
        in_specs=[vmem] * len(terms),
        out_specs=[vmem] * len(out_shapes),
        scratch_shapes=scratch,
        compiler_params=pltpu.CompilerParams(
            collective_id=1, has_side_effects=True, vmem_limit_bytes=60 << 20
        ),
        name="reduce_all",
    )(*terms)


def norm_forward(inputs):
    center = inputs - jnp.mean(inputs, axis=-1, keepdims=True)
    inverse = lax.rsqrt(jnp.mean(center * center, axis=-1, keepdims=True) + epsilon)
    return (center * inverse, inverse)


def norm_backward(grad_hat, normed, inverse):
    mean_grad = jnp.mean(grad_hat, axis=-1, keepdims=True)
    mean_cross = jnp.mean(grad_hat * normed, axis=-1, keepdims=True)
    return inverse * (grad_hat - mean_grad - normed * mean_cross)


def rotation(token_pos, head_dim):
    half_dim = head_dim // 2
    frequency = rope_base ** (-(jnp.arange(half_dim, dtype=jnp.float32) * 2.0 / head_dim))
    angles = token_pos.astype(jnp.float32)[:, None] * frequency[None, :]
    return (jnp.cos(angles)[:, None, :], jnp.sin(angles)[:, None, :])


def rotate(inputs, cosine_part, sine_part):
    half_dim = inputs.shape[-1] // 2
    upper = inputs[..., :half_dim]
    lower = inputs[..., half_dim:]
    return jnp.concatenate(
        [upper * cosine_part - lower * sine_part, lower * cosine_part + upper * sine_part], axis=-1
    )


def unrotate(grads, cosine_part, sine_part):
    half_dim = grads.shape[-1] // 2
    upper = grads[..., :half_dim]
    lower = grads[..., half_dim:]
    return jnp.concatenate(
        [upper * cosine_part + lower * sine_part, lower * cosine_part - upper * sine_part], axis=-1
    )


def gelu_parts(pre_act):
    normal_cdf = 0.5 * (1.0 + lax.erf(pre_act * 0.7071067811865476))
    normal_pdf = jnp.exp(-0.5 * pre_act * pre_act) * 0.3989422804014327
    return (pre_act * normal_cdf, normal_cdf + pre_act * normal_pdf)


def band_mask(query_ids, key_ids):
    query_count = query_ids.shape[0]
    key_count = key_ids.shape[0]
    window_reach = (key_count - query_count) // 2
    offsets = jnp.arange(query_count)[:, None] + window_reach - jnp.arange(key_count)[None, :]
    return (jnp.abs(offsets) <= window_reach) & (query_ids[:, None] == key_ids[None, :])


def attend(queries, key_rows, value_rows, allowed, score_scale):
    scores = (
        jnp.einsum("qhd,khd->hqk", queries, key_rows, preferred_element_type=jnp.float32)
        * score_scale
    )
    scores = jnp.where(allowed[None], scores, -1e30)
    log_total = jnp.log(jnp.sum(jnp.exp(scores), axis=-1))
    attn_probs = jnp.exp(scores - log_total[..., None]).astype(jnp.bfloat16)
    return (
        jnp.einsum("hqk,khd->qhd", attn_probs, value_rows, preferred_element_type=jnp.float32),
        log_total,
    )


def attend_back(queries, key_rows, value_rows, allowed, log_total, grad_out, score_scale):
    scores = (
        jnp.einsum("qhd,khd->hqk", queries, key_rows, preferred_element_type=jnp.float32)
        * score_scale
    )
    probs_full = jnp.where(allowed[None], jnp.exp(scores - log_total[..., None]), 0.0)
    grad_probs = jnp.einsum(
        "qhd,khd->hqk", grad_out, value_rows, preferred_element_type=jnp.float32
    )
    row_delta = jnp.sum(probs_full * grad_probs, axis=-1, keepdims=True)
    grad_scores = (probs_full * (grad_probs - row_delta) * score_scale).astype(jnp.bfloat16)
    grad_query = jnp.einsum(
        "hqk,khd->qhd", grad_scores, key_rows, preferred_element_type=jnp.float32
    )
    grad_keys = jnp.einsum("hqk,qhd->khd", grad_scores, queries, preferred_element_type=jnp.float32)
    grad_values = jnp.einsum(
        "hqk,qhd->khd",
        probs_full.astype(jnp.bfloat16),
        grad_out,
        preferred_element_type=jnp.float32,
    )
    return (grad_query, grad_keys, grad_values)


def local(
    block_in,
    seq_ids,
    positions,
    attn_gain,
    qkv_weight,
    attn_out_weight,
    mlp_gain,
    mlp_in_weight,
    mlp_out_weight,
    cotangent,
):
    shard_width = attn_gain.shape[0]
    lanes = -(-shard_width // 128) * 128
    gain_rows = jnp.pad(
        jnp.stack([attn_gain, mlp_gain]), ((0, 30), (0, lanes - shard_width))
    )
    w_qkv, gains, w_attn_out, w_mlp_in, w_mlp_out = gather_all(
        (qkv_weight, gain_rows, attn_out_weight, mlp_in_weight, mlp_out_weight)
    )
    gains = gains.reshape(4, 32, lanes)[:, :2, :shard_width].transpose(1, 0, 2).reshape(2, -1)
    gain_full_one, gain_full_two = gains[0], gains[1]
    tok_rows, model_width = block_in.shape
    head_count = model_width // HD
    hidden_units = w_mlp_out.shape[0]
    score_scale = HD ** (-0.5)
    ext_rows = tok_rows + 2 * W
    query_block = 128
    block_count = tok_rows // query_block
    window_rows = query_block + 2 * W
    gain_one = gain_full_one.astype(jnp.float32)
    gain_two = gain_full_two.astype(jnp.float32)
    inputs = block_in.astype(jnp.float32)
    normed_one, inverse_one = norm_forward(inputs)
    normed_in = (normed_one * gain_one).astype(jnp.bfloat16)
    packed_qkv = jnp.dot(normed_in, w_qkv, preferred_element_type=jnp.float32)
    cosine_part, sine_part = rotation(positions, HD)
    queries = rotate(
        packed_qkv[:, :model_width].reshape(tok_rows, head_count, HD), cosine_part, sine_part
    ).astype(jnp.bfloat16)
    own_keys = rotate(
        packed_qkv[:, model_width : 2 * model_width].reshape(tok_rows, head_count, HD),
        cosine_part,
        sine_part,
    ).astype(jnp.bfloat16)
    own_values = packed_qkv[:, 2 * model_width :].astype(jnp.bfloat16)
    keys_values = jnp.concatenate([own_keys.reshape(tok_rows, model_width), own_values], axis=1)
    key_ids = seq_ids + 1
    prev_kv, prev_ids = shifted(
        (keys_values[tok_rows - W :], key_ids[tok_rows - W :]), ("seq", "fsdp"), 1
    )
    next_kv, next_ids = shifted((keys_values[:W], key_ids[:W]), ("seq", "fsdp"), -1)
    ext_kv = jnp.concatenate([prev_kv, keys_values, next_kv], axis=0)
    ext_ids = jnp.concatenate([prev_ids, key_ids, next_ids], axis=0)
    block_keys = []
    block_values = []
    block_masks = []
    attn_parts = []
    log_parts = []
    for block in range(block_count):
        begin = block * query_block
        window_kv = ext_kv[begin : begin + window_rows]
        key_rows = window_kv[:, :model_width].reshape(window_rows, head_count, HD)
        value_rows = window_kv[:, model_width:].reshape(window_rows, head_count, HD)
        allowed = band_mask(
            key_ids[begin : begin + query_block], ext_ids[begin : begin + window_rows]
        )
        attn_block, log_block = attend(
            queries[begin : begin + query_block], key_rows, value_rows, allowed, score_scale
        )
        block_keys.append(key_rows)
        block_values.append(value_rows)
        block_masks.append(allowed)
        attn_parts.append(attn_block)
        log_parts.append(log_block)
    attn_flat = (
        jnp.concatenate(attn_parts, axis=0).reshape(tok_rows, model_width).astype(jnp.bfloat16)
    )
    hidden_one = inputs + jnp.dot(attn_flat, w_attn_out, preferred_element_type=jnp.float32)
    normed_two, inverse_two = norm_forward(hidden_one)
    normed_mid = (normed_two * gain_two).astype(jnp.bfloat16)
    up_rows = jnp.dot(normed_mid, w_mlp_in, preferred_element_type=jnp.float32)
    gelu_value, gelu_slope = gelu_parts(up_rows[:, :hidden_units])
    gate_rows = up_rows[:, hidden_units:]
    mixed = (gelu_value * gate_rows).astype(jnp.bfloat16)
    block_out = (hidden_one + jnp.dot(mixed, w_mlp_out, preferred_element_type=jnp.float32)).astype(
        jnp.bfloat16
    )
    mlp_out_term = jnp.dot(mixed.T, cotangent, preferred_element_type=jnp.float32)
    grad_mixed = jnp.dot(cotangent, w_mlp_out.T, preferred_element_type=jnp.float32)
    grad_up = jnp.concatenate(
        [grad_mixed * gate_rows * gelu_slope, grad_mixed * gelu_value], axis=1
    ).astype(jnp.bfloat16)
    mlp_in_term = jnp.dot(normed_mid.T, grad_up, preferred_element_type=jnp.float32)
    grad_normed_two = jnp.dot(grad_up, w_mlp_in.T, preferred_element_type=jnp.float32)
    gain_two_term = jnp.sum(grad_normed_two * normed_two, axis=0)
    grad_hidden = cotangent.astype(jnp.float32) + norm_backward(
        grad_normed_two * gain_two, normed_two, inverse_two
    )
    grad_hidden_b = grad_hidden.astype(jnp.bfloat16)
    attn_out_term = jnp.dot(attn_flat.T, grad_hidden_b, preferred_element_type=jnp.float32)
    grad_attn = (
        jnp.dot(grad_hidden_b, w_attn_out.T, preferred_element_type=jnp.float32)
        .astype(jnp.bfloat16)
        .reshape(tok_rows, head_count, HD)
    )
    query_parts = []
    key_grads = jnp.zeros((ext_rows, 2 * model_width), jnp.float32)
    for block in range(block_count):
        begin = block * query_block
        grad_query_block, grad_keys, grad_values = attend_back(
            queries[begin : begin + query_block],
            block_keys[block],
            block_values[block],
            block_masks[block],
            log_parts[block],
            grad_attn[begin : begin + query_block],
            score_scale,
        )
        query_parts.append(grad_query_block)
        window_grads = jnp.concatenate(
            [
                grad_keys.reshape(window_rows, model_width),
                grad_values.reshape(window_rows, model_width),
            ],
            axis=1,
        )
        key_grads = key_grads + jnp.pad(
            window_grads, ((begin, ext_rows - begin - window_rows), (0, 0))
        )
    grad_query = jnp.concatenate(query_parts, axis=0)
    from_next = shifted(key_grads[:W].astype(jnp.bfloat16), ("seq", "fsdp"), -1).astype(jnp.float32)
    from_prev = shifted(key_grads[ext_rows - W :].astype(jnp.bfloat16), ("seq", "fsdp"), 1).astype(
        jnp.float32
    )
    own_grads = key_grads[W : W + tok_rows]
    own_grads = (
        own_grads
        + jnp.pad(from_prev, ((0, tok_rows - W), (0, 0)))
        + jnp.pad(from_next, ((tok_rows - W, 0), (0, 0)))
    )
    grad_q = unrotate(grad_query, cosine_part, sine_part).reshape(tok_rows, model_width)
    grad_k = unrotate(
        own_grads[:, :model_width].reshape(tok_rows, head_count, HD), cosine_part, sine_part
    ).reshape(tok_rows, model_width)
    grad_qkv = jnp.concatenate([grad_q, grad_k, own_grads[:, model_width:]], axis=1).astype(
        jnp.bfloat16
    )
    qkv_term = jnp.dot(normed_in.T, grad_qkv, preferred_element_type=jnp.float32)
    grad_normed_one = jnp.dot(grad_qkv, w_qkv.T, preferred_element_type=jnp.float32)
    gain_one_term = jnp.sum(grad_normed_one * normed_one, axis=0)
    input_grad = grad_hidden + norm_backward(grad_normed_one * gain_one, normed_one, inverse_one)
    gain_terms = jnp.stack([gain_one_term, gain_two_term]).astype(jnp.bfloat16)
    gain_terms = gain_terms.reshape(2, 4, shard_width).transpose(1, 0, 2)
    gain_terms = jnp.pad(gain_terms, ((0, 0), (0, 62), (0, lanes - shard_width)))
    terms = (
        mlp_out_term.astype(jnp.bfloat16),
        gain_terms.reshape(4 * 64, lanes),
        mlp_in_term.astype(jnp.bfloat16),
        attn_out_term.astype(jnp.bfloat16),
        qkv_term.astype(jnp.bfloat16),
    )
    chunks = []
    for at, term in enumerate(terms):
        rows, columns = term.shape[0] // 4, term.shape[1]
        width = model_width if columns % model_width == 0 else columns
        for begin in range(0, columns, width):
            chunks.append((at, begin, width, rows, at, begin))
    out_shapes = [(term.shape[0] // 4, term.shape[1]) for term in terms]
    out_shapes[1] = (16, lanes)
    sums = reduce_all(terms, out_shapes, chunks)
    results = (
        sums[1][0, :shard_width], sums[4], sums[3], sums[1][1, :shard_width], sums[2], sums[0]
    )
    return (
        block_out,
        input_grad,
        results[0],
        results[1],
        results[2],
        results[3],
        results[4],
        results[5],
    )


def solution(mesh):
    in_specs = (
        P(("seq", "fsdp"), None),
        P(("seq", "fsdp")),
        P(("seq", "fsdp")),
        P("fsdp"),
        P("fsdp", None),
        P("fsdp", None),
        P("fsdp"),
        P("fsdp", None),
        P("fsdp", None),
        P(("seq", "fsdp"), None),
    )
    out_specs = (
        P(("seq", "fsdp"), None),
        P(("seq", "fsdp"), None),
        P("fsdp"),
        P("fsdp", None),
        P("fsdp", None),
        P("fsdp"),
        P("fsdp", None),
        P("fsdp", None),
    )
    return jax.shard_map(local, mesh=mesh, in_specs=in_specs, out_specs=out_specs, check_vma=False)
```

```python
import functools

import jax
import jax.numpy as jnp
from jax import lax
from jax.experimental import pallas as pl
from jax.experimental.pallas import tpu as pltpu
from jax.sharding import PartitionSpec as P

HD = 64
W = 64


epsilon = 1e-05
rope_base = 10000.0


def shifted(array, axis, by):
    size = lax.axis_size(axis)
    pairs = [(i, i + by) for i in range(size) if 0 <= i + by < size]
    return lax.ppermute(array, axis, pairs)


def places():
    fsdp_at = lax.axis_index("fsdp")
    seq_at = lax.axis_index("seq")
    chip_x = fsdp_at // 2
    core = lax.rem(fsdp_at, 2)
    return fsdp_at, seq_at, chip_x, core


def flipped(index, bit):
    flag = lax.rem(index // bit, 2)
    return index + bit - 2 * bit * flag


def greet(partners):
    barrier = pltpu.get_barrier_semaphore()
    for name, at in partners:
        pl.semaphore_signal(
            barrier, inc=1, device_id={name: at}, device_id_type=pl.DeviceIdType.MESH
        )
    pl.semaphore_wait(barrier, len(partners))


def remote(src, dst, send, recv, name, at):
    return pltpu.make_async_remote_copy(
        src_ref=src,
        dst_ref=dst,
        send_sem=send,
        recv_sem=recv,
        device_id={name: at},
        device_id_type=pl.DeviceIdType.MESH,
    )


def gather_kernel(count, *refs):
    shards = refs[:count]
    wholes = refs[count : 2 * count]
    send, recv, local_sem = refs[2 * count :]
    fsdp_at, seq_at, chip_x, core = places()
    side = lax.rem(seq_at, 2)
    beside = flipped(fsdp_at, 1)
    across = flipped(fsdp_at, 2)
    far = flipped(across, 1)
    next_y = flipped(seq_at, 1)
    greet((("fsdp", beside), ("fsdp", across), ("seq", next_y)))

    def rows_of(k, owner, half):
        rows = shards[k].shape[0]
        if half is None:
            return wholes[k].at[pl.ds(pl.multiple_of(owner * rows, 16), rows)]
        begin = owner * rows + half * (rows // 2)
        return wholes[k].at[pl.ds(pl.multiple_of(begin, 16), rows // 2)]

    def mine(k):
        rows = shards[k].shape[0] // 2
        return shards[k].at[pl.ds(pl.multiple_of(side * rows, 16), rows)]

    copies = []
    x_copies = []
    for k in range(count):
        copy = remote(
            mine(k), rows_of(k, fsdp_at, side), send.at[k, 0], recv.at[k, 0], "fsdp", across
        )
        copy.start()
        x_copies.append(copy)
    for k in range(count):
        copy = remote(
            shards[k], rows_of(k, fsdp_at, None), send.at[k, 1], recv.at[k, 1], "fsdp", beside
        )
        copy.start()
        copies.append(copy)
    for k in range(count):
        pltpu.make_async_copy(shards[k], rows_of(k, fsdp_at, None), local_sem.at[k]).start()
    y_copies = []

    def pass_on(k):
        y_copies[k].wait_recv()
        half = rows_of(k, across, 1 - side)
        copy = remote(half, half, send.at[k, 4], recv.at[k, 4], "fsdp", beside)
        copy.start()
        copies.append(copy)

    for k in range(count):
        x_copies[k].wait_recv()
        half = rows_of(k, across, side)
        copy = remote(half, half, send.at[k, 2], recv.at[k, 2], "seq", next_y)
        copy.start()
        y_copies.append(copy)
        copy = remote(half, half, send.at[k, 3], recv.at[k, 3], "fsdp", beside)
        copy.start()
        copies.append(copy)
        if k > 0:
            pass_on(k - 1)
    pass_on(count - 1)
    for k in range(count):
        pltpu.make_async_copy(shards[k], rows_of(k, fsdp_at, None), local_sem.at[k]).wait()
    for copy in copies:
        copy.wait()
    for copy in x_copies + y_copies:
        copy.wait_send()


def gather_all(shards):
    count = len(shards)
    vmem = pl.BlockSpec(memory_space=pltpu.VMEM)
    return pl.pallas_call(
        functools.partial(gather_kernel, count),
        out_shape=[
            jax.ShapeDtypeStruct((4 * shard.shape[0], shard.shape[1]), shard.dtype)
            for shard in shards
        ],
        in_specs=[vmem] * count,
        out_specs=[vmem] * count,
        scratch_shapes=[
            pltpu.SemaphoreType.DMA((count, 5)),
            pltpu.SemaphoreType.DMA((count, 5)),
            pltpu.SemaphoreType.DMA((count,)),
        ],
        compiler_params=pltpu.CompilerParams(
            collective_id=0, has_side_effects=True, vmem_limit_bytes=40 << 20
        ),
        name="gather_all",
    )(*shards)


def add_into(dst, left, right):
    rows = dst.shape[0]
    block = 48 if rows % 48 == 0 else 16

    def step(i, carry):
        at = pl.ds(pl.multiple_of(i * block, 16), block)
        total = left[at].astype(jnp.float32) + right[at].astype(jnp.float32)
        dst[at] = total.astype(dst.dtype)
        return carry

    lax.fori_loop(0, rows // block, step, 0)


def reduce_kernel(chunks, outputs, bits, *refs):
    inputs = max(chunk[0] for chunk in chunks) + 1
    ins = refs[:inputs]
    outs = refs[inputs : inputs + outputs]
    rest = refs[inputs + outputs :]
    n = len(chunks)
    from_core = rest[:n]
    from_x = rest[n : 2 * n]
    from_y = rest[2 * n : 3 * n]
    from_z = rest[3 * n : 4 * n]
    from_far = rest[4 * n : 5 * n]
    final = rest[5 * n : 6 * n]
    send, recv = rest[6 * n :]
    fsdp_at, seq_at, chip_x, core = places()
    y = lax.rem(seq_at, 2)
    z = lax.rem(seq_at // 2, 2)
    beside = flipped(fsdp_at, 1)
    across = flipped(fsdp_at, 2)
    next_y = flipped(seq_at, 1)
    next_z = flipped(seq_at, 2)
    far = [flipped(seq_at, bit) for bit in bits]
    greet(
        [("fsdp", beside), ("fsdp", across), ("seq", next_y), ("seq", next_z)]
        + [("seq", at) for at in far]
    )

    def owner_rows(k, owner):
        source, begin, columns, rows = chunks[k][:4]
        at = pl.ds(pl.multiple_of(owner * rows, 16), rows)
        return ins[source].at[at, pl.ds(begin, columns)]

    def y_half(ref, flag):
        rows = ref.shape[0] // 2
        return ref.at[pl.ds(pl.multiple_of(flag * rows, 16), rows)]

    def z_half(ref, flag):
        rows, columns = ref.shape
        if rows % 32 == 0:
            return ref.at[pl.ds(pl.multiple_of(flag * (rows // 2), 16), rows // 2)]
        return ref.at[:, pl.ds(pl.multiple_of(flag * (columns // 2), 128), columns // 2)]

    started = []
    arriving = {}

    def go(k, slot, src, dst, name, at):
        copy = remote(src, dst, send.at[k, slot], recv.at[k, slot], name, at)
        copy.start()
        started.append(copy)
        arriving[k, slot] = copy

    def core_send(k):
        for far_x in range(2):
            go(
                k, far_x, owner_rows(k, 2 * far_x + 1 - core), from_core[k].at[far_x],
                "fsdp", beside,
            )

    def x_send(k):
        for far_x in range(2):
            arriving[k, far_x].wait_recv()
            spot = from_core[k].at[far_x]
            add_into(spot, spot, owner_rows(k, 2 * far_x + core))
        go(k, 2, from_core[k].at[1 - chip_x], from_x[k], "fsdp", across)

    def y_send(k):
        arriving[k, 2].wait_recv()
        add_into(from_x[k], from_x[k], from_core[k].at[chip_x])
        go(k, 3, y_half(from_x[k], 1 - y), from_y[k], "seq", next_y)

    def z_send(k):
        arriving[k, 3].wait_recv()
        add_into(from_y[k], from_y[k], y_half(from_x[k], y))
        go(k, 4, z_half(from_y[k], 1 - z), from_z[k], "seq", next_z)

    def spot(k):
        return z_half(y_half(final[k], y), z)

    def far_send(level):
        def stage(k):
            if level == 0:
                arriving[k, 4].wait_recv()
                source = from_z[k]
                add_into(source, source, z_half(from_y[k], z))
            else:
                arriving[k, 6 + level].wait_recv()
                source = from_far[k].at[level - 1]
                before = from_z[k] if level == 1 else from_far[k].at[level - 2]
                add_into(source, source, before)
            go(k, 7 + level, source, from_far[k].at[level], "seq", far[level])

        return stage

    def z_back(k):
        if bits:
            level = len(bits) - 1
            arriving[k, 7 + level].wait_recv()
            before = from_z[k] if level == 0 else from_far[k].at[level - 1]
            add_into(spot(k), from_far[k].at[level], before)
        else:
            arriving[k, 4].wait_recv()
            add_into(spot(k), from_z[k], z_half(from_y[k], z))
        go(k, 5, spot(k), spot(k), "seq", next_z)

    def y_back(k):
        arriving[k, 5].wait_recv()
        half = y_half(final[k], y)
        go(k, 6, half, half, "seq", next_y)

    def finish(k):
        arriving[k, 6].wait_recv()
        out, begin, columns = chunks[k][4], chunks[k][5], chunks[k][2]
        rows = outs[out].shape[0]
        block = 48 if rows % 48 == 0 else 16

        def step(i, carry):
            at = pl.ds(pl.multiple_of(i * block, 16), block)
            outs[out][at, pl.ds(begin, columns)] = final[k][at].astype(jnp.float32)
            return carry

        lax.fori_loop(0, rows // block, step, 0)

    stages = [y_send, z_send] + [far_send(i) for i in range(len(bits))] + [z_back, y_back, finish]
    for k in range(n):
        core_send(k)
    for wave in range(n + len(stages) + 1):
        if wave < n:
            x_send(wave)
        for lag in reversed(range(len(stages))):
            k = wave - 2 - lag
            if 0 <= k < n:
                stages[lag](k)
    for copy in started:
        copy.wait_send()


def reduce_all(terms, out_shapes, chunks):
    seq_size = lax.axis_size("seq")
    assert lax.axis_size("fsdp") == 4 and seq_size >= 4 and seq_size & (seq_size - 1) == 0
    bits = []
    while (4 << len(bits)) < seq_size:
        bits.append(4 << len(bits))
    n = len(chunks)
    vmem = pl.BlockSpec(memory_space=pltpu.VMEM)
    halves = []
    quarters = []
    for chunk in chunks:
        columns, rows = chunk[2], chunk[3]
        halves.append((rows // 2, columns))
        quarters.append((rows // 4, columns) if rows % 64 == 0 else (rows // 2, columns // 2))
    scratch = (
        [pltpu.VMEM((2, c[3], c[2]), jnp.bfloat16) for c in chunks]
        + [pltpu.VMEM((c[3], c[2]), jnp.bfloat16) for c in chunks]
        + [pltpu.VMEM(h, jnp.bfloat16) for h in halves]
        + [pltpu.VMEM(q, jnp.bfloat16) for q in quarters]
        + [pltpu.VMEM((max(len(bits), 1),) + q, jnp.bfloat16) for q in quarters]
        + [pltpu.VMEM((c[3], c[2]), jnp.bfloat16) for c in chunks]
        + [pltpu.SemaphoreType.DMA((n, 7 + len(bits)))] * 2
    )
    return pl.pallas_call(
        functools.partial(reduce_kernel, chunks, len(out_shapes), bits),
        out_shape=[jax.ShapeDtypeStruct(shape, jnp.float32) for shape in out_shapes],
        in_specs=[vmem] * len(terms),
        out_specs=[vmem] * len(out_shapes),
        scratch_shapes=scratch,
        compiler_params=pltpu.CompilerParams(
            collective_id=1, has_side_effects=True, vmem_limit_bytes=60 << 20
        ),
        name="reduce_all",
    )(*terms)


def norm_forward(inputs):
    center = inputs - jnp.mean(inputs, axis=-1, keepdims=True)
    inverse = lax.rsqrt(jnp.mean(center * center, axis=-1, keepdims=True) + epsilon)
    return (center * inverse, inverse)


def norm_backward(grad_hat, normed, inverse):
    mean_grad = jnp.mean(grad_hat, axis=-1, keepdims=True)
    mean_cross = jnp.mean(grad_hat * normed, axis=-1, keepdims=True)
    return inverse * (grad_hat - mean_grad - normed * mean_cross)


def rotation(token_pos, head_dim):
    half_dim = head_dim // 2
    frequency = rope_base ** (-(jnp.arange(half_dim, dtype=jnp.float32) * 2.0 / head_dim))
    angles = token_pos.astype(jnp.float32)[:, None] * frequency[None, :]
    cosine, sine = jnp.cos(angles), jnp.sin(angles)
    copies = 128 // head_dim
    return (
        jnp.concatenate([cosine, cosine] * copies, axis=1),
        jnp.concatenate([-sine, sine] * copies, axis=1),
    )


def gelu_parts(pre_act):
    normal_cdf = 0.5 * (1.0 + lax.erf(pre_act * 0.7071067811865476))
    normal_pdf = jnp.exp(-0.5 * pre_act * pre_act) * 0.3989422804014327
    return (pre_act * normal_cdf, normal_cdf + pre_act * normal_pdf)


def swap_halves(u):
    lane = lax.broadcasted_iota(jnp.int32, u.shape, 1)
    quarter = HD // 2
    width = u.shape[1]
    ahead = pltpu.roll(u, width - quarter, 1)
    behind = pltpu.roll(u, quarter, 1)
    return jnp.where(lane % HD < quarter, ahead, behind)


def project_kernel(h_ref, w_ref, cos_ref, sin_ref, q_ref, kv_ref):
    width = q_ref.shape[1]
    block = 256
    cos, sin = cos_ref[...], sin_ref[...]
    for begin in range(0, 3 * width, block):
        u = jnp.dot(
            h_ref[...], w_ref[:, begin : begin + block], preferred_element_type=jnp.float32
        )
        for at in range(0, block, 128):
            part = u[:, at : at + 128]
            column = begin + at
            if column < 2 * width:
                part = part * cos + swap_halves(part) * sin
            part = part.astype(jnp.bfloat16)
            if column < width:
                q_ref[:, column : column + 128] = part
            else:
                kv_ref[:, column - width : column - width + 128] = part


def block_mask(q_ids, k_ids):
    rows, columns = q_ids.shape[0], k_ids.shape[1]
    reach = (columns - rows) // 2
    i = lax.broadcasted_iota(jnp.int32, (rows, columns), 0)
    j = lax.broadcasted_iota(jnp.int32, (rows, columns), 1)
    return (jnp.abs(i + reach - j) <= reach) & (q_ids == k_ids)


def dot_nt(left, right):
    return lax.dot_general(
        left, right, (((1,), (1,)), ((), ())), preferred_element_type=jnp.float32
    )


def dot_tn(left, right):
    return lax.dot_general(
        left, right, (((0,), (0,)), ((), ())), preferred_element_type=jnp.float32
    )


def only_head(array, head):
    lane = lax.broadcasted_iota(jnp.int32, array.shape, 1)
    return jnp.where(lane // HD == head, array, jnp.zeros_like(array))


def attn_kernel(scale, q_ref, kv_ref, q_ids_ref, k_ids_ref, out_ref):
    tok_rows, width = q_ref.shape
    rows = 128
    window = rows + 2 * W

    def pair(p, carry):
        at = pl.ds(pl.multiple_of(p * 128, 128), 128)
        v_at = pl.ds(pl.multiple_of(width + p * 128, 128), 128)
        for begin in range(0, tok_rows, rows):
            q = q_ref[begin : begin + rows, at]
            k = kv_ref[begin : begin + window, at]
            v = kv_ref[begin : begin + window, v_at]
            allowed = block_mask(
                q_ids_ref[begin : begin + rows, :], k_ids_ref[:, begin : begin + window]
            )
            total = jnp.zeros((rows, 128), jnp.float32)
            for head in range(128 // HD):
                scores = dot_nt(only_head(q, head), k) * scale
                scores = jnp.where(allowed, scores, -1e30)
                log_total = jnp.log(jnp.sum(jnp.exp(scores), axis=1, keepdims=True))
                probs = jnp.exp(scores - log_total).astype(jnp.bfloat16)
                out = jnp.dot(probs, v, preferred_element_type=jnp.float32)
                total = total + only_head(out, head)
            out_ref[begin : begin + rows, at] = total.astype(jnp.bfloat16)
        return carry

    lax.fori_loop(0, width // 128, pair, 0)


def attn_back_kernel(
    scale, q_ref, kv_ref, q_ids_ref, k_ids_ref, g_ref, cos_ref, sin_ref, gq_ref, gkv_ref
):
    tok_rows, width = q_ref.shape
    rows = 128
    window = rows + 2 * W

    def pair(p, carry):
        at = pl.ds(pl.multiple_of(p * 128, 128), 128)
        v_at = pl.ds(pl.multiple_of(width + p * 128, 128), 128)
        for begin in range(0, tok_rows, rows):
            q = q_ref[begin : begin + rows, at]
            g = g_ref[begin : begin + rows, at]
            k = kv_ref[begin : begin + window, at]
            v = kv_ref[begin : begin + window, v_at]
            allowed = block_mask(
                q_ids_ref[begin : begin + rows, :], k_ids_ref[:, begin : begin + window]
            )
            gq = jnp.zeros((rows, 128), jnp.float32)
            gk = jnp.zeros((window, 128), jnp.float32)
            gv = jnp.zeros((window, 128), jnp.float32)
            for head in range(128 // HD):
                q_head = only_head(q, head)
                g_head = only_head(g, head)
                scores = dot_nt(q_head, k) * scale
                scores = jnp.where(allowed, scores, -1e30)
                log_total = jnp.log(jnp.sum(jnp.exp(scores), axis=1, keepdims=True))
                probs = jnp.where(allowed, jnp.exp(scores - log_total), 0.0)
                gp = dot_nt(g_head, v)
                delta = jnp.sum(probs * gp, axis=1, keepdims=True)
                gs = (probs * (gp - delta) * scale).astype(jnp.bfloat16)
                gq = gq + only_head(jnp.dot(gs, k, preferred_element_type=jnp.float32), head)
                gk = gk + dot_tn(gs, q_head)
                gv = gv + dot_tn(probs.astype(jnp.bfloat16), g_head)
            cos = cos_ref[begin : begin + rows, :]
            sin = sin_ref[begin : begin + rows, :]
            gq_ref[begin : begin + rows, at] = (gq * cos - swap_halves(gq) * sin).astype(
                jnp.bfloat16
            )
            old = 0 if begin == 0 else window - rows
            if old:
                gkv_ref[begin : begin + old, at] += gk[:old]
                gkv_ref[begin : begin + old, v_at] += gv[:old]
            gkv_ref[begin + old : begin + window, at] = gk[old:]
            gkv_ref[begin + old : begin + window, v_at] = gv[old:]
        return carry

    lax.fori_loop(0, width // 128, pair, 0)


def join_kernel(gq_ref, gkv_ref, prev_ref, next_ref, cos_ref, sin_ref, out_ref):
    tok_rows, width = gq_ref.shape
    out_ref[:, :width] = gq_ref[...]
    cos, sin = cos_ref[...], sin_ref[...]
    for column in range(0, 2 * width, 128):
        at = slice(column, column + 128)
        top = gkv_ref[W : 2 * W, at] + prev_ref[:, at].astype(jnp.float32)
        middle = gkv_ref[2 * W : tok_rows, at]
        low = gkv_ref[tok_rows : tok_rows + W, at] + next_ref[:, at].astype(jnp.float32)
        grad = jnp.concatenate([top, middle, low], axis=0)
        if column < width:
            grad = grad * cos - swap_halves(grad) * sin
        out_ref[:, width + column : width + column + 128] = grad.astype(jnp.bfloat16)


def on_core(kernel, name, out_shape, flops, *args):
    vmem = pl.BlockSpec(memory_space=pltpu.VMEM)
    many = isinstance(out_shape, list)
    return pl.pallas_call(
        kernel,
        out_shape=out_shape,
        in_specs=[vmem] * len(args),
        out_specs=[vmem] * len(out_shape) if many else vmem,
        compiler_params=pltpu.CompilerParams(vmem_limit_bytes=32 << 20),
        cost_estimate=pl.CostEstimate(flops=flops, bytes_accessed=8 << 20, transcendentals=0),
        name=name,
    )(*args)


def local(
    block_in,
    seq_ids,
    positions,
    attn_gain,
    qkv_weight,
    attn_out_weight,
    mlp_gain,
    mlp_in_weight,
    mlp_out_weight,
    cotangent,
):
    shard_width = attn_gain.shape[0]
    lanes = -(-shard_width // 128) * 128
    gain_rows = jnp.pad(
        jnp.stack([attn_gain, mlp_gain]), ((0, 30), (0, lanes - shard_width))
    )
    w_qkv, gains, w_attn_out, w_mlp_in, w_mlp_out = gather_all(
        (qkv_weight, gain_rows, attn_out_weight, mlp_in_weight, mlp_out_weight)
    )
    gains = gains.reshape(4, 32, lanes)[:, :2, :shard_width].transpose(1, 0, 2).reshape(2, -1)
    gain_full_one, gain_full_two = gains[0], gains[1]
    tok_rows, model_width = block_in.shape
    hidden_units = w_mlp_out.shape[0]
    score_scale = HD ** (-0.5)
    ext_rows = tok_rows + 2 * W
    gain_one = gain_full_one.astype(jnp.float32)
    gain_two = gain_full_two.astype(jnp.float32)
    inputs = block_in.astype(jnp.float32)
    normed_one, inverse_one = norm_forward(inputs)
    normed_in = (normed_one * gain_one).astype(jnp.bfloat16)
    cosine_part, sine_part = rotation(positions, HD)
    queries, keys_values = on_core(
        project_kernel,
        "project",
        [
            jax.ShapeDtypeStruct((tok_rows, model_width), jnp.bfloat16),
            jax.ShapeDtypeStruct((tok_rows, 2 * model_width), jnp.bfloat16),
        ],
        6 * tok_rows * model_width * model_width,
        normed_in,
        w_qkv,
        cosine_part,
        sine_part,
    )
    key_ids = seq_ids + 1
    prev_kv, prev_ids = shifted(
        (keys_values[tok_rows - W :], key_ids[tok_rows - W :]), ("seq", "fsdp"), 1
    )
    next_kv, next_ids = shifted((keys_values[:W], key_ids[:W]), ("seq", "fsdp"), -1)
    ext_kv = jnp.concatenate([prev_kv, keys_values, next_kv], axis=0)
    ext_ids = jnp.concatenate([prev_ids, key_ids, next_ids], axis=0)
    query_ids = key_ids[:, None]
    ext_ids = ext_ids[None, :]
    attn_flat = on_core(
        functools.partial(attn_kernel, score_scale),
        "attn",
        jax.ShapeDtypeStruct((tok_rows, model_width), jnp.bfloat16),
        8 * tok_rows * 256 * model_width,
        queries,
        ext_kv,
        query_ids,
        ext_ids,
    )
    hidden_one = inputs + jnp.dot(attn_flat, w_attn_out, preferred_element_type=jnp.float32)
    normed_two, inverse_two = norm_forward(hidden_one)
    normed_mid = (normed_two * gain_two).astype(jnp.bfloat16)
    up_rows = jnp.dot(normed_mid, w_mlp_in, preferred_element_type=jnp.float32)
    gelu_value, gelu_slope = gelu_parts(up_rows[:, :hidden_units])
    gate_rows = up_rows[:, hidden_units:]
    mixed = (gelu_value * gate_rows).astype(jnp.bfloat16)
    block_out = (hidden_one + jnp.dot(mixed, w_mlp_out, preferred_element_type=jnp.float32)).astype(
        jnp.bfloat16
    )
    mlp_out_term = jnp.dot(mixed.T, cotangent, preferred_element_type=jnp.float32)
    grad_mixed = jnp.dot(cotangent, w_mlp_out.T, preferred_element_type=jnp.float32)
    grad_up = jnp.concatenate(
        [grad_mixed * gate_rows * gelu_slope, grad_mixed * gelu_value], axis=1
    ).astype(jnp.bfloat16)
    mlp_in_term = jnp.dot(normed_mid.T, grad_up, preferred_element_type=jnp.float32)
    grad_normed_two = jnp.dot(grad_up, w_mlp_in.T, preferred_element_type=jnp.float32)
    gain_two_term = jnp.sum(grad_normed_two * normed_two, axis=0)
    grad_hidden = cotangent.astype(jnp.float32) + norm_backward(
        grad_normed_two * gain_two, normed_two, inverse_two
    )
    grad_hidden_b = grad_hidden.astype(jnp.bfloat16)
    attn_out_term = jnp.dot(attn_flat.T, grad_hidden_b, preferred_element_type=jnp.float32)
    grad_attn = jnp.dot(
        grad_hidden_b, w_attn_out.T, preferred_element_type=jnp.float32
    ).astype(jnp.bfloat16)
    grad_query, key_grads = on_core(
        functools.partial(attn_back_kernel, score_scale),
        "attn_back",
        [
            jax.ShapeDtypeStruct((tok_rows, model_width), jnp.bfloat16),
            jax.ShapeDtypeStruct((ext_rows, 2 * model_width), jnp.float32),
        ],
        20 * tok_rows * 256 * model_width,
        queries,
        ext_kv,
        query_ids,
        ext_ids,
        grad_attn,
        cosine_part,
        sine_part,
    )
    from_next = shifted(key_grads[:W].astype(jnp.bfloat16), ("seq", "fsdp"), -1)
    from_prev = shifted(key_grads[ext_rows - W :].astype(jnp.bfloat16), ("seq", "fsdp"), 1)
    grad_qkv = on_core(
        join_kernel,
        "join",
        jax.ShapeDtypeStruct((tok_rows, 3 * model_width), jnp.bfloat16),
        1 << 20,
        grad_query,
        key_grads,
        from_prev,
        from_next,
        cosine_part,
        sine_part,
    )
    qkv_term = jnp.dot(normed_in.T, grad_qkv, preferred_element_type=jnp.float32)
    grad_normed_one = jnp.dot(grad_qkv, w_qkv.T, preferred_element_type=jnp.float32)
    gain_one_term = jnp.sum(grad_normed_one * normed_one, axis=0)
    input_grad = grad_hidden + norm_backward(grad_normed_one * gain_one, normed_one, inverse_one)
    gain_terms = jnp.stack([gain_one_term, gain_two_term]).astype(jnp.bfloat16)
    gain_terms = gain_terms.reshape(2, 4, shard_width).transpose(1, 0, 2)
    gain_terms = jnp.pad(gain_terms, ((0, 0), (0, 62), (0, lanes - shard_width)))
    terms = (
        mlp_out_term.astype(jnp.bfloat16),
        gain_terms.reshape(4 * 64, lanes),
        mlp_in_term.astype(jnp.bfloat16),
        attn_out_term.astype(jnp.bfloat16),
        qkv_term.astype(jnp.bfloat16),
    )
    chunks = []
    for at, term in enumerate(terms):
        rows, columns = term.shape[0] // 4, term.shape[1]
        width = model_width if columns % model_width == 0 else columns
        if at == 4:
            width = model_width // 2
        for begin in range(0, columns, width):
            chunks.append((at, begin, width, rows, at, begin))
    out_shapes = [(term.shape[0] // 4, term.shape[1]) for term in terms]
    out_shapes[1] = (16, lanes)
    sums = reduce_all(terms, out_shapes, chunks)
    results = (
        sums[1][0, :shard_width], sums[4], sums[3], sums[1][1, :shard_width], sums[2], sums[0]
    )
    return (
        block_out,
        input_grad,
        results[0],
        results[1],
        results[2],
        results[3],
        results[4],
        results[5],
    )


def solution(mesh):
    in_specs = (
        P(("seq", "fsdp"), None),
        P(("seq", "fsdp")),
        P(("seq", "fsdp")),
        P("fsdp"),
        P("fsdp", None),
        P("fsdp", None),
        P("fsdp"),
        P("fsdp", None),
        P("fsdp", None),
        P(("seq", "fsdp"), None),
    )
    out_specs = (
        P(("seq", "fsdp"), None),
        P(("seq", "fsdp"), None),
        P("fsdp"),
        P("fsdp", None),
        P("fsdp", None),
        P("fsdp"),
        P("fsdp", None),
        P("fsdp", None),
    )
    return jax.shard_map(local, mesh=mesh, in_specs=in_specs, out_specs=out_specs, check_vma=False)
```

```python
import functools
import heapq

import jax
import jax.numpy as jnp
from jax import lax
from jax.experimental import pallas as pl
from jax.experimental.pallas import tpu as pltpu
from jax.sharding import PartitionSpec as P

HD = 64
W = 64


epsilon = 1e-05
rope_base = 10000.0


def shifted(array, axis, by):
    size = lax.axis_size(axis)
    pairs = [(i, i + by) for i in range(size) if 0 <= i + by < size]
    return lax.ppermute(array, axis, pairs)


def places():
    fsdp_at = lax.axis_index("fsdp")
    seq_at = lax.axis_index("seq")
    chip_x = fsdp_at // 2
    core = lax.rem(fsdp_at, 2)
    return fsdp_at, seq_at, chip_x, core


def flipped(index, bit):
    flag = lax.rem(index // bit, 2)
    return index + bit - 2 * bit * flag


def greet(partners):
    barrier = pltpu.get_barrier_semaphore()
    for name, at in partners:
        pl.semaphore_signal(
            barrier, inc=1, device_id={name: at}, device_id_type=pl.DeviceIdType.MESH
        )
    pl.semaphore_wait(barrier, len(partners))


def remote(src, dst, send, recv, name, at):
    return pltpu.make_async_remote_copy(
        src_ref=src,
        dst_ref=dst,
        send_sem=send,
        recv_sem=recv,
        device_id={name: at},
        device_id_type=pl.DeviceIdType.MESH,
    )


def gather_kernel(count, pieces, *refs):
    shards = refs[:count]
    wholes = refs[count : 2 * count]
    send, recv, local_sem = refs[2 * count :]
    fsdp_at, seq_at, chip_x, core = places()
    side = lax.rem(seq_at, 2)
    beside = flipped(fsdp_at, 1)
    across = flipped(fsdp_at, 2)
    far = flipped(across, 1)
    next_y = flipped(seq_at, 1)
    greet((("fsdp", beside), ("fsdp", across), ("seq", next_y)))

    def rows_of(piece, owner, half):
        source, first, columns = piece
        rows = shards[source].shape[0]
        begin = owner * rows
        if half is not None:
            rows = rows // 2
            begin = begin + half * rows
        at = pl.ds(pl.multiple_of(begin, 16), rows)
        return wholes[source].at[at, pl.ds(first, columns)]

    def own(piece, half):
        source, first, columns = piece
        rows = shards[source].shape[0]
        if half is None:
            return shards[source].at[:, pl.ds(first, columns)]
        at = pl.ds(pl.multiple_of(half * (rows // 2), 16), rows // 2)
        return shards[source].at[at, pl.ds(first, columns)]

    copies = []
    x_copies = []
    for k, piece in enumerate(pieces):
        copy = remote(
            own(piece, side), rows_of(piece, fsdp_at, side), send.at[k, 0], recv.at[k, 0],
            "fsdp", across,
        )
        copy.start()
        x_copies.append(copy)
    for k, piece in enumerate(pieces):
        copy = remote(
            own(piece, None), rows_of(piece, fsdp_at, None), send.at[k, 1], recv.at[k, 1],
            "fsdp", beside,
        )
        copy.start()
        copies.append(copy)
    local_copies = []
    for k in range(count):
        whole = (k, 0, shards[k].shape[1])
        copy = pltpu.make_async_copy(shards[k], rows_of(whole, fsdp_at, None), local_sem.at[k])
        copy.start()
        local_copies.append(copy)
    y_copies = []

    def pass_on(k):
        y_copies[k].wait_recv()
        half = rows_of(pieces[k], across, 1 - side)
        copy = remote(half, half, send.at[k, 4], recv.at[k, 4], "fsdp", beside)
        copy.start()
        copies.append(copy)

    for k in range(len(pieces)):
        x_copies[k].wait_recv()
        half = rows_of(pieces[k], across, side)
        copy = remote(half, half, send.at[k, 2], recv.at[k, 2], "seq", next_y)
        copy.start()
        y_copies.append(copy)
        copy = remote(half, half, send.at[k, 3], recv.at[k, 3], "fsdp", beside)
        copy.start()
        copies.append(copy)
        if k > 0:
            pass_on(k - 1)
    pass_on(len(pieces) - 1)
    for copy in local_copies + copies:
        copy.wait()
    for copy in x_copies + y_copies:
        copy.wait_send()


def gather_all(shards):
    count = len(shards)
    pieces = []
    for at, shard in enumerate(shards):
        columns = shard.shape[1]
        cuts = 3 if columns % 768 == 0 and columns > 768 else 2 if columns % 256 == 0 else 1
        if shard.shape[0] < 64:
            cuts = 1
        for i in range(cuts):
            pieces.append((at, i * (columns // cuts), columns // cuts))
    vmem = pl.BlockSpec(memory_space=pltpu.VMEM)
    return pl.pallas_call(
        functools.partial(gather_kernel, count, pieces),
        out_shape=[
            jax.ShapeDtypeStruct((4 * shard.shape[0], shard.shape[1]), shard.dtype)
            for shard in shards
        ],
        in_specs=[vmem] * count,
        out_specs=[vmem] * count,
        scratch_shapes=[
            pltpu.SemaphoreType.DMA((len(pieces), 5)),
            pltpu.SemaphoreType.DMA((len(pieces), 5)),
            pltpu.SemaphoreType.DMA((count,)),
        ],
        compiler_params=pltpu.CompilerParams(
            collective_id=0, has_side_effects=True, vmem_limit_bytes=40 << 20
        ),
        name="gather_all",
    )(*shards)


def add_into(dst, left, right):
    rows = dst.shape[0]
    block = 48 if rows % 48 == 0 else 16

    def step(i, carry):
        at = pl.ds(pl.multiple_of(i * block, 16), block)
        total = left[at].astype(jnp.float32) + right[at].astype(jnp.float32)
        dst[at] = total.astype(dst.dtype)
        return carry

    lax.fori_loop(0, rows // block, step, 0)


def planned_order(chunks, bits):
    shares = [1.0, 0.5, 0.25] + [0.25 * (bit // 2) for bit in bits] + [0.25, 0.5]
    links = ["x", "y", "z"] + [("far", bit) for bit in bits] + ["z", "y"]
    free = {}
    events = []
    at_core = 0.0
    for k, chunk in enumerate(chunks):
        size = 2 * chunk[2] * chunk[3]
        at_core += 2 * size / 200e3
        heapq.heappush(events, (at_core + 2.0, k, 0))
    order = []
    now = 0.0
    while events:
        ready, k, stage = heapq.heappop(events)
        now = max(now, ready) + 0.3
        order.append((k, stage))
        if stage < len(links):
            size = 2 * chunks[k][2] * chunks[k][3] * shares[stage]
            begin = max(now, free.get(links[stage], 0.0))
            free[links[stage]] = begin + size / 45e3
            heapq.heappush(events, (free[links[stage]] + 2.0, k, stage + 1))
    return order


def reduce_kernel(chunks, outputs, bits, *refs):
    inputs = max(chunk[0] for chunk in chunks) + 1
    ins = refs[:inputs]
    outs = refs[inputs : inputs + outputs]
    rest = refs[inputs + outputs :]
    n = len(chunks)
    from_core = rest[:n]
    from_x = rest[n : 2 * n]
    from_y = rest[2 * n : 3 * n]
    from_z = rest[3 * n : 4 * n]
    from_far = rest[4 * n : 5 * n]
    send, recv = rest[5 * n :]
    final = [outs[c[4]].at[:, pl.ds(c[5], c[2])] for c in chunks]
    fsdp_at, seq_at, chip_x, core = places()
    y = lax.rem(seq_at, 2)
    z = lax.rem(seq_at // 2, 2)
    beside = flipped(fsdp_at, 1)
    across = flipped(fsdp_at, 2)
    next_y = flipped(seq_at, 1)
    next_z = flipped(seq_at, 2)
    far = [flipped(seq_at, bit) for bit in bits]
    greet(
        [("fsdp", beside), ("fsdp", across), ("seq", next_y), ("seq", next_z)]
        + [("seq", at) for at in far]
    )

    def owner_rows(k, owner):
        source, begin, columns, rows = chunks[k][:4]
        at = pl.ds(pl.multiple_of(owner * rows, 16), rows)
        return ins[source].at[at, pl.ds(begin, columns)]

    def y_half(ref, flag):
        rows = ref.shape[0] // 2
        return ref.at[pl.ds(pl.multiple_of(flag * rows, 16), rows)]

    def z_half(ref, flag):
        rows, columns = ref.shape
        if rows % 32 == 0:
            return ref.at[pl.ds(pl.multiple_of(flag * (rows // 2), 16), rows // 2)]
        return ref.at[:, pl.ds(pl.multiple_of(flag * (columns // 2), 128), columns // 2)]

    started = []
    arriving = {}

    def go(k, slot, src, dst, name, at):
        copy = remote(src, dst, send.at[k, slot], recv.at[k, slot], name, at)
        copy.start()
        started.append(copy)
        arriving[k, slot] = copy

    def core_send(k):
        for far_x in range(2):
            go(
                k, far_x, owner_rows(k, 2 * far_x + 1 - core), from_core[k].at[far_x],
                "fsdp", beside,
            )

    def x_send(k):
        for far_x in range(2):
            arriving[k, far_x].wait_recv()
            spot = from_core[k].at[far_x]
            add_into(spot, spot, owner_rows(k, 2 * far_x + core))
        go(k, 2, from_core[k].at[1 - chip_x], from_x[k], "fsdp", across)

    def y_send(k):
        arriving[k, 2].wait_recv()
        add_into(from_x[k], from_x[k], from_core[k].at[chip_x])
        go(k, 3, y_half(from_x[k], 1 - y), from_y[k], "seq", next_y)

    def z_send(k):
        arriving[k, 3].wait_recv()
        add_into(from_y[k], from_y[k], y_half(from_x[k], y))
        go(k, 4, z_half(from_y[k], 1 - z), from_z[k], "seq", next_z)

    def spot(k):
        return z_half(y_half(final[k], y), z)

    def far_send(level):
        def stage(k):
            if level == 0:
                arriving[k, 4].wait_recv()
                source = from_z[k]
                add_into(source, source, z_half(from_y[k], z))
            else:
                arriving[k, 6 + level].wait_recv()
                source = from_far[k].at[level - 1]
                before = from_z[k] if level == 1 else from_far[k].at[level - 2]
                add_into(source, source, before)
            go(k, 7 + level, source, from_far[k].at[level], "seq", far[level])

        return stage

    def z_back(k):
        if bits:
            level = len(bits) - 1
            arriving[k, 7 + level].wait_recv()
            before = from_z[k] if level == 0 else from_far[k].at[level - 1]
            add_into(spot(k), from_far[k].at[level], before)
        else:
            arriving[k, 4].wait_recv()
            add_into(spot(k), from_z[k], z_half(from_y[k], z))
        go(k, 5, spot(k), spot(k), "seq", next_z)

    def y_back(k):
        arriving[k, 5].wait_recv()
        half = y_half(final[k], y)
        go(k, 6, half, half, "seq", next_y)

    def finish(k):
        arriving[k, 6].wait_recv()

    stages = [x_send, y_send, z_send]
    stages += [far_send(i) for i in range(len(bits))] + [z_back, y_back, finish]
    for k in range(n):
        core_send(k)
    for k, stage in planned_order(chunks, bits):
        stages[stage](k)
    for copy in started:
        copy.wait_send()


def reduce_all(terms, out_shapes, chunks):
    seq_size = lax.axis_size("seq")
    assert lax.axis_size("fsdp") == 4 and seq_size >= 4 and seq_size & (seq_size - 1) == 0
    bits = []
    while (4 << len(bits)) < seq_size:
        bits.append(4 << len(bits))
    n = len(chunks)
    vmem = pl.BlockSpec(memory_space=pltpu.VMEM)
    halves = []
    quarters = []
    for chunk in chunks:
        columns, rows = chunk[2], chunk[3]
        halves.append((rows // 2, columns))
        quarters.append((rows // 4, columns) if rows % 64 == 0 else (rows // 2, columns // 2))
    scratch = (
        [pltpu.VMEM((2, c[3], c[2]), jnp.bfloat16) for c in chunks]
        + [pltpu.VMEM((c[3], c[2]), jnp.bfloat16) for c in chunks]
        + [pltpu.VMEM(h, jnp.bfloat16) for h in halves]
        + [pltpu.VMEM(q, jnp.bfloat16) for q in quarters]
        + [pltpu.VMEM((max(len(bits), 1),) + q, jnp.bfloat16) for q in quarters]
        + [pltpu.SemaphoreType.DMA((n, 7 + len(bits)))] * 2
    )
    return pl.pallas_call(
        functools.partial(reduce_kernel, chunks, len(out_shapes), bits),
        out_shape=[jax.ShapeDtypeStruct(shape, jnp.bfloat16) for shape in out_shapes],
        in_specs=[vmem] * len(terms),
        out_specs=[vmem] * len(out_shapes),
        scratch_shapes=scratch,
        compiler_params=pltpu.CompilerParams(
            collective_id=1, has_side_effects=True, vmem_limit_bytes=60 << 20
        ),
        name="reduce_all",
    )(*terms)


def norm_forward(inputs):
    center = inputs - jnp.mean(inputs, axis=-1, keepdims=True)
    inverse = lax.rsqrt(jnp.mean(center * center, axis=-1, keepdims=True) + epsilon)
    return (center * inverse, inverse)


def norm_backward(grad_hat, normed, inverse):
    mean_grad = jnp.mean(grad_hat, axis=-1, keepdims=True)
    mean_cross = jnp.mean(grad_hat * normed, axis=-1, keepdims=True)
    return inverse * (grad_hat - mean_grad - normed * mean_cross)


def rotation(token_pos, head_dim):
    half_dim = head_dim // 2
    frequency = rope_base ** (-(jnp.arange(half_dim, dtype=jnp.float32) * 2.0 / head_dim))
    angles = token_pos.astype(jnp.float32)[:, None] * frequency[None, :]
    cosine, sine = jnp.cos(angles), jnp.sin(angles)
    copies = 128 // head_dim
    return (
        jnp.concatenate([cosine, cosine] * copies, axis=1),
        jnp.concatenate([-sine, sine] * copies, axis=1),
    )


def gelu_parts(pre_act):
    normal_cdf = 0.5 * (1.0 + lax.erf(pre_act * 0.7071067811865476))
    normal_pdf = jnp.exp(-0.5 * pre_act * pre_act) * 0.3989422804014327
    return (pre_act * normal_cdf, normal_cdf + pre_act * normal_pdf)


def swap_halves(u):
    lane = lax.broadcasted_iota(jnp.int32, u.shape, 1)
    quarter = HD // 2
    width = u.shape[1]
    ahead = pltpu.roll(u, width - quarter, 1)
    behind = pltpu.roll(u, quarter, 1)
    return jnp.where(lane % HD < quarter, ahead, behind)


def project_kernel(h_ref, w_ref, cos_ref, sin_ref, q_ref, kv_ref):
    width = q_ref.shape[1]
    block = 256
    cos, sin = cos_ref[...], sin_ref[...]
    for begin in range(0, 3 * width, block):
        u = jnp.dot(
            h_ref[...], w_ref[:, begin : begin + block], preferred_element_type=jnp.float32
        )
        for at in range(0, block, 128):
            part = u[:, at : at + 128]
            column = begin + at
            if column < 2 * width:
                part = part * cos + swap_halves(part) * sin
            part = part.astype(jnp.bfloat16)
            if column < width:
                q_ref[:, column : column + 128] = part
            else:
                kv_ref[:, column - width : column - width + 128] = part


def block_mask(q_ids, k_ids):
    rows, columns = q_ids.shape[0], k_ids.shape[1]
    reach = (columns - rows) // 2
    i = lax.broadcasted_iota(jnp.int32, (rows, columns), 0)
    j = lax.broadcasted_iota(jnp.int32, (rows, columns), 1)
    return (jnp.abs(i + reach - j) <= reach) & (q_ids == k_ids)


def dot_nt(left, right):
    return lax.dot_general(
        left, right, (((1,), (1,)), ((), ())), preferred_element_type=jnp.float32
    )


def dot_tn(left, right):
    return lax.dot_general(
        left, right, (((0,), (0,)), ((), ())), preferred_element_type=jnp.float32
    )


def only_head(array, head):
    lane = lax.broadcasted_iota(jnp.int32, array.shape, 1)
    return jnp.where(lane // HD == head, array, jnp.zeros_like(array))


def attn_kernel(scale, q_ref, kv_ref, q_ids_ref, k_ids_ref, out_ref):
    tok_rows, width = q_ref.shape
    rows = 128
    window = rows + 2 * W

    def pair(p, carry):
        at = pl.ds(pl.multiple_of(p * 128, 128), 128)
        v_at = pl.ds(pl.multiple_of(width + p * 128, 128), 128)
        for begin in range(0, tok_rows, rows):
            q = q_ref[begin : begin + rows, at]
            k = kv_ref[begin : begin + window, at]
            v = kv_ref[begin : begin + window, v_at]
            allowed = block_mask(
                q_ids_ref[begin : begin + rows, :], k_ids_ref[:, begin : begin + window]
            )
            total = jnp.zeros((rows, 128), jnp.float32)
            for head in range(128 // HD):
                scores = dot_nt(only_head(q, head), k) * scale
                scores = jnp.where(allowed, scores, -1e30)
                log_total = jnp.log(jnp.sum(jnp.exp(scores), axis=1, keepdims=True))
                probs = jnp.exp(scores - log_total).astype(jnp.bfloat16)
                out = jnp.dot(probs, v, preferred_element_type=jnp.float32)
                total = total + only_head(out, head)
            out_ref[begin : begin + rows, at] = total.astype(jnp.bfloat16)
        return carry

    lax.fori_loop(0, width // 128, pair, 0)


def attn_back_kernel(
    scale, q_ref, kv_ref, q_ids_ref, k_ids_ref, g_ref, cos_ref, sin_ref, gq_ref, gkv_ref
):
    tok_rows, width = q_ref.shape
    rows = 128
    window = rows + 2 * W

    def pair(p, carry):
        at = pl.ds(pl.multiple_of(p * 128, 128), 128)
        v_at = pl.ds(pl.multiple_of(width + p * 128, 128), 128)
        for begin in range(0, tok_rows, rows):
            q = q_ref[begin : begin + rows, at]
            g = g_ref[begin : begin + rows, at]
            k = kv_ref[begin : begin + window, at]
            v = kv_ref[begin : begin + window, v_at]
            allowed = block_mask(
                q_ids_ref[begin : begin + rows, :], k_ids_ref[:, begin : begin + window]
            )
            gq = jnp.zeros((rows, 128), jnp.float32)
            gk = jnp.zeros((window, 128), jnp.float32)
            gv = jnp.zeros((window, 128), jnp.float32)
            for head in range(128 // HD):
                q_head = only_head(q, head)
                g_head = only_head(g, head)
                scores = dot_nt(q_head, k) * scale
                scores = jnp.where(allowed, scores, -1e30)
                log_total = jnp.log(jnp.sum(jnp.exp(scores), axis=1, keepdims=True))
                probs = jnp.where(allowed, jnp.exp(scores - log_total), 0.0)
                gp = dot_nt(g_head, v)
                delta = jnp.sum(probs * gp, axis=1, keepdims=True)
                gs = (probs * (gp - delta) * scale).astype(jnp.bfloat16)
                gq = gq + only_head(jnp.dot(gs, k, preferred_element_type=jnp.float32), head)
                gk = gk + dot_tn(gs, q_head)
                gv = gv + dot_tn(probs.astype(jnp.bfloat16), g_head)
            cos = cos_ref[begin : begin + rows, :]
            sin = sin_ref[begin : begin + rows, :]
            gq_ref[begin : begin + rows, at] = (gq * cos - swap_halves(gq) * sin).astype(
                jnp.bfloat16
            )
            old = 0 if begin == 0 else window - rows
            if old:
                gkv_ref[begin : begin + old, at] += gk[:old]
                gkv_ref[begin : begin + old, v_at] += gv[:old]
            gkv_ref[begin + old : begin + window, at] = gk[old:]
            gkv_ref[begin + old : begin + window, v_at] = gv[old:]
        return carry

    lax.fori_loop(0, width // 128, pair, 0)


def join_kernel(gq_ref, gkv_ref, prev_ref, next_ref, cos_ref, sin_ref, out_ref):
    tok_rows, width = gq_ref.shape
    out_ref[:, :width] = gq_ref[...]
    cos, sin = cos_ref[...], sin_ref[...]
    for column in range(0, 2 * width, 128):
        at = slice(column, column + 128)
        top = gkv_ref[W : 2 * W, at] + prev_ref[:, at].astype(jnp.float32)
        middle = gkv_ref[2 * W : tok_rows, at]
        low = gkv_ref[tok_rows : tok_rows + W, at] + next_ref[:, at].astype(jnp.float32)
        grad = jnp.concatenate([top, middle, low], axis=0)
        if column < width:
            grad = grad * cos - swap_halves(grad) * sin
        out_ref[:, width + column : width + column + 128] = grad.astype(jnp.bfloat16)


def on_core(kernel, name, out_shape, flops, *args):
    vmem = pl.BlockSpec(memory_space=pltpu.VMEM)
    many = isinstance(out_shape, list)
    return pl.pallas_call(
        kernel,
        out_shape=out_shape,
        in_specs=[vmem] * len(args),
        out_specs=[vmem] * len(out_shape) if many else vmem,
        compiler_params=pltpu.CompilerParams(vmem_limit_bytes=32 << 20),
        cost_estimate=pl.CostEstimate(flops=flops, bytes_accessed=8 << 20, transcendentals=0),
        name=name,
    )(*args)


def local(
    block_in,
    seq_ids,
    positions,
    attn_gain,
    qkv_weight,
    attn_out_weight,
    mlp_gain,
    mlp_in_weight,
    mlp_out_weight,
    cotangent,
):
    shard_width = attn_gain.shape[0]
    lanes = -(-shard_width // 128) * 128
    gain_rows = jnp.pad(
        jnp.stack([attn_gain, mlp_gain]), ((0, 30), (0, lanes - shard_width))
    )
    w_qkv, gains, w_mlp_in, w_mlp_out, w_attn_out = gather_all(
        (qkv_weight, gain_rows, mlp_in_weight, mlp_out_weight, attn_out_weight)
    )
    gains = gains.reshape(4, 32, lanes)[:, :2, :shard_width].transpose(1, 0, 2).reshape(2, -1)
    gain_full_one, gain_full_two = gains[0], gains[1]
    tok_rows, model_width = block_in.shape
    hidden_units = w_mlp_out.shape[0]
    score_scale = HD ** (-0.5)
    ext_rows = tok_rows + 2 * W
    gain_one = gain_full_one.astype(jnp.float32)
    gain_two = gain_full_two.astype(jnp.float32)
    inputs = block_in.astype(jnp.float32)
    normed_one, inverse_one = norm_forward(inputs)
    normed_in = (normed_one * gain_one).astype(jnp.bfloat16)
    cosine_part, sine_part = rotation(positions, HD)
    queries, keys_values = on_core(
        project_kernel,
        "project",
        [
            jax.ShapeDtypeStruct((tok_rows, model_width), jnp.bfloat16),
            jax.ShapeDtypeStruct((tok_rows, 2 * model_width), jnp.bfloat16),
        ],
        6 * tok_rows * model_width * model_width,
        normed_in,
        w_qkv,
        cosine_part,
        sine_part,
    )
    key_ids = seq_ids + 1
    prev_kv, prev_ids = shifted(
        (keys_values[tok_rows - W :], key_ids[tok_rows - W :]), ("seq", "fsdp"), 1
    )
    next_kv, next_ids = shifted((keys_values[:W], key_ids[:W]), ("seq", "fsdp"), -1)
    ext_kv = jnp.concatenate([prev_kv, keys_values, next_kv], axis=0)
    ext_ids = jnp.concatenate([prev_ids, key_ids, next_ids], axis=0)
    query_ids = key_ids[:, None]
    ext_ids = ext_ids[None, :]
    attn_flat = on_core(
        functools.partial(attn_kernel, score_scale),
        "attn",
        jax.ShapeDtypeStruct((tok_rows, model_width), jnp.bfloat16),
        8 * tok_rows * 256 * model_width,
        queries,
        ext_kv,
        query_ids,
        ext_ids,
    )
    hidden_one = inputs + jnp.dot(attn_flat, w_attn_out, preferred_element_type=jnp.float32)
    normed_two, inverse_two = norm_forward(hidden_one)
    normed_mid = (normed_two * gain_two).astype(jnp.bfloat16)
    up_rows = jnp.dot(normed_mid, w_mlp_in, preferred_element_type=jnp.float32)
    gelu_value, gelu_slope = gelu_parts(up_rows[:, :hidden_units])
    gate_rows = up_rows[:, hidden_units:]
    mixed = (gelu_value * gate_rows).astype(jnp.bfloat16)
    block_out = (hidden_one + jnp.dot(mixed, w_mlp_out, preferred_element_type=jnp.float32)).astype(
        jnp.bfloat16
    )
    mlp_out_term = jnp.dot(mixed.T, cotangent, preferred_element_type=jnp.float32)
    grad_mixed = jnp.dot(cotangent, w_mlp_out.T, preferred_element_type=jnp.float32)
    grad_up = jnp.concatenate(
        [grad_mixed * gate_rows * gelu_slope, grad_mixed * gelu_value], axis=1
    ).astype(jnp.bfloat16)
    mlp_in_term = jnp.dot(normed_mid.T, grad_up, preferred_element_type=jnp.float32)
    grad_normed_two = jnp.dot(grad_up, w_mlp_in.T, preferred_element_type=jnp.float32)
    gain_two_term = jnp.sum(grad_normed_two * normed_two, axis=0)
    grad_hidden = cotangent.astype(jnp.float32) + norm_backward(
        grad_normed_two * gain_two, normed_two, inverse_two
    )
    grad_hidden_b = grad_hidden.astype(jnp.bfloat16)
    attn_out_term = jnp.dot(attn_flat.T, grad_hidden_b, preferred_element_type=jnp.float32)
    grad_attn = jnp.dot(
        grad_hidden_b, w_attn_out.T, preferred_element_type=jnp.float32
    ).astype(jnp.bfloat16)
    grad_query, key_grads = on_core(
        functools.partial(attn_back_kernel, score_scale),
        "attn_back",
        [
            jax.ShapeDtypeStruct((tok_rows, model_width), jnp.bfloat16),
            jax.ShapeDtypeStruct((ext_rows, 2 * model_width), jnp.float32),
        ],
        20 * tok_rows * 256 * model_width,
        queries,
        ext_kv,
        query_ids,
        ext_ids,
        grad_attn,
        cosine_part,
        sine_part,
    )
    from_next = shifted(key_grads[:W].astype(jnp.bfloat16), ("seq", "fsdp"), -1)
    from_prev = shifted(key_grads[ext_rows - W :].astype(jnp.bfloat16), ("seq", "fsdp"), 1)
    grad_qkv = on_core(
        join_kernel,
        "join",
        jax.ShapeDtypeStruct((tok_rows, 3 * model_width), jnp.bfloat16),
        1 << 20,
        grad_query,
        key_grads,
        from_prev,
        from_next,
        cosine_part,
        sine_part,
    )
    qkv_term = jnp.dot(normed_in.T, grad_qkv, preferred_element_type=jnp.float32)
    grad_normed_one = jnp.dot(grad_qkv, w_qkv.T, preferred_element_type=jnp.float32)
    gain_one_term = jnp.sum(grad_normed_one * normed_one, axis=0)
    input_grad = grad_hidden + norm_backward(grad_normed_one * gain_one, normed_one, inverse_one)
    gain_terms = jnp.stack([gain_one_term, gain_two_term]).astype(jnp.bfloat16)
    gain_terms = gain_terms.reshape(2, 4, shard_width).transpose(1, 0, 2)
    gain_terms = jnp.pad(gain_terms, ((0, 0), (0, 62), (0, lanes - shard_width)))
    terms = (
        attn_out_term.astype(jnp.bfloat16),
        mlp_in_term.astype(jnp.bfloat16),
        mlp_out_term.astype(jnp.bfloat16),
        gain_terms.reshape(4 * 64, lanes),
        qkv_term.astype(jnp.bfloat16),
    )
    chunks = []
    for at, term in enumerate(terms):
        rows, columns = term.shape[0] // 4, term.shape[1]
        width = columns
        if columns % 768 == 0:
            width = 384 if rows % 64 == 0 else 256
        for begin in range(0, columns, width):
            chunks.append((at, begin, width, rows, at, begin))
    out_shapes = [(term.shape[0] // 4, term.shape[1]) for term in terms]
    sums = [total.astype(jnp.float32) for total in reduce_all(terms, out_shapes, chunks)]
    results = (
        sums[3][0, :shard_width], sums[4], sums[0], sums[3][1, :shard_width], sums[1], sums[2]
    )
    return (
        block_out,
        input_grad,
        results[0],
        results[1],
        results[2],
        results[3],
        results[4],
        results[5],
    )


def solution(mesh):
    in_specs = (
        P(("seq", "fsdp"), None),
        P(("seq", "fsdp")),
        P(("seq", "fsdp")),
        P("fsdp"),
        P("fsdp", None),
        P("fsdp", None),
        P("fsdp"),
        P("fsdp", None),
        P("fsdp", None),
        P(("seq", "fsdp"), None),
    )
    out_specs = (
        P(("seq", "fsdp"), None),
        P(("seq", "fsdp"), None),
        P("fsdp"),
        P("fsdp", None),
        P("fsdp", None),
        P("fsdp"),
        P("fsdp", None),
        P("fsdp", None),
    )
    return jax.shard_map(local, mesh=mesh, in_specs=in_specs, out_specs=out_specs, check_vma=False)
```
